256 devices in a mesh: row: 16 (over z_lo, x), col: 16 (over z_hi, y, core).
Axes of the slice: x: 4, y: 4, z: 8 (z_hi: 2, z_lo: 4; z = z_hi * 4 + z_lo), core: 2. Of those that a mesh axis runs over, the one named last changes fastest.
Arguments:
- start_vector: float32 [12288, 12288], P('row', 'col'), may hold values from -6 to 6, as said below
- ham_blocks: bfloat16 [768, 128, 128], P('row'), may hold values from -0.1875 to 0.1875
- diagonal: float32 [12288], replicated, may hold values from -1 to 1
- pair_lists: int32 [3, 16, 64], replicated, may hold values from 0 to 47, as said below
- pair_counts: int32 [16], replicated, may hold values from 16 to 64, as said below
- hot_blocks: int32 [16, 2], replicated, may hold values from 0 to 5, as said below
- selection: int32 [16, 16], replicated, may hold values from 0 to 1
Outputs:
- first_iterate: float32 [12288, 12288], P('row', 'col')
- second_iterate: float32 [12288, 12288], P('row', 'col')
The draws below stay inside these ranges and needn't reach their ends.
Inputs may be any that keep to these rules, and one draw needn't show every extreme that they name: start_vector is symmetric: entry (a, b) equals entry (b, a). `pair_lists`: component 0 is a tile (0 to 15), component 1 a block of a tile (0 to 5), component 2 a block id (0 to 47); slot k < 16 of every list has source tile k. `pair_counts`: some tile has all 64 slots live. `hot_blocks`: the 2 blocks of a tile are distinct.
All inputs are finite; a program needn't handle non-finite values.
Results may differ from the reference program's by a relative error of at most 0.0023.
Values may be sent and summed in bfloat16 or wider, within the bound.
No kernel may reach another device: no remote copies, remote signals or barrier semaphores. Data moves between devices by JAX's collectives and lax.ppermute only.
A program may use at most 128 MiB of HBM per device.

```python
import jax
import jax.numpy as jnp
from jax import lax

N = 12288
BLK = 128
HOT = 2
NPAIR = 64
NHB = 48
NTILE = 16
BT = 6


def draw_start_vector(key, part):
    base = jax.random.normal(key, (N, N), jnp.float32)
    return jnp.clip((base + base.T) * 0.7071067811865476, -6.0, 6.0)


def draw_pair_lists(key, part):
    key_source, key_target, key_ham = jax.random.split(jax.random.fold_in(key, 11), 3)
    pair_shape = (NTILE, NPAIR)
    random_source = jax.random.randint(key_source, pair_shape, 0, NTILE)
    position = jnp.arange(NPAIR, dtype=jnp.int32)[None, :] + jnp.zeros((NTILE, 1), jnp.int32)
    source = jnp.where(position < NTILE, position, random_source)
    target = jax.random.randint(key_target, pair_shape, 0, BT)
    ham_ids = jax.random.randint(key_ham, pair_shape, 0, NHB)
    return jnp.stack([source, target, ham_ids]).astype(jnp.int32)


def draw_pair_counts(key, part):
    lowest = max(NTILE, NPAIR // 4)
    spread_size = NPAIR - lowest
    first_key, second_key, third_key = jax.random.split(jax.random.fold_in(key, 13), 3)
    first_draw = jax.random.randint(first_key, (NTILE,), 0, spread_size + 1)
    second_draw = jax.random.randint(second_key, (NTILE,), 0, spread_size + 1)
    drawn = lowest + first_draw * second_draw // max(spread_size, 1)
    busiest = jax.random.randint(third_key, (), 0, NTILE)
    return jnp.where(jnp.arange(NTILE) == busiest, NPAIR, drawn).astype(jnp.int32)


def draw_hot_blocks(key, part):
    scores = jax.random.randint(jax.random.fold_in(key, 17), (NTILE, BT), 0, 1 << 20) * BT + jnp.arange(BT, dtype=jnp.int32)[None, :]
    ordering = jnp.argsort(scores, axis=1)
    return ordering[:, :HOT].astype(jnp.int32)


def plant(result, stream_key, low, largest):
    longest = result.shape.index(max(result.shape))
    spots = []
    for shift in (0, 1):
        where = [jax.random.randint(jax.random.fold_in(stream_key, axis), (), 0, length) for axis, length in enumerate(result.shape)]
        where[longest] = (where[longest] + shift) % result.shape[longest]
        spots.append(tuple(where))
    return result.at[spots[0]].set(low).at[spots[1]].set(largest)


def block_scale(stream_key, shape, cuts, low, largest):
    loudness = 1.0
    for axis_at, blocks in cuts:
        heights = jax.random.uniform(jax.random.fold_in(jax.random.fold_in(stream_key, 6), axis_at), (blocks,), jnp.float32, low / len(cuts), largest / len(cuts))
        loudness = loudness * jnp.repeat(jnp.exp(heights), shape[axis_at] // blocks).reshape((-1,) + (1,) * (len(shape) - 1 - axis_at))
    return loudness


def centred(key, dims, deviation, most, cuts=(), kind=jnp.bfloat16):
    array = deviation * jax.random.normal(key, dims, jnp.float32)
    if cuts:
        array = array * block_scale(key, dims, cuts, -0.22, 0.18)
    return jnp.clip(array, -most, most).astype(kind)


def setup_inputs(seed: int = 0) -> dict:
    seeds = jax.random.split(jax.random.key(seed), 8)
    return {
        "start_vector": draw_start_vector(jax.random.fold_in(seeds[7], 71), 0),
        "ham_blocks": centred(seeds[1], (NTILE * NHB, BLK, BLK), (BLK * 8) ** -0.5, 0.1875, ((0, 16),)),
        "diagonal": jnp.clip(jax.random.uniform(seeds[2], (N,), jnp.float32, -1.0, 1.0), -1.0, 1.0),
        "pair_lists": draw_pair_lists(jax.random.fold_in(seeds[7], 71), 0),
        "pair_counts": draw_pair_counts(jax.random.fold_in(seeds[7], 71), 0),
        "hot_blocks": draw_hot_blocks(jax.random.fold_in(seeds[7], 71), 0),
        "selection": plant(jax.random.randint(seeds[6], (NTILE, NTILE), 0, HOT), jax.random.fold_in(seeds[6], 1), 0, HOT - 1).astype(jnp.int32),
    }


center = 0.25
half_width = 2.5


def operator(iterate, ham_blocks, diagonal, pair_lists, pair_counts, hot_blocks, selection):
    tile_rows = N // NTILE
    rounded = lax.optimization_barrier(iterate.astype(jnp.bfloat16)).astype(jnp.float32)
    ham_wide = ham_blocks.astype(jnp.float32)

    def update(flat_index, accumulated):
        target_tile = flat_index // NPAIR
        pair_index = flat_index % NPAIR
        source_tile = pair_lists[0, target_tile, pair_index]
        target_block = pair_lists[1, target_tile, pair_index]
        block_id = pair_lists[2, target_tile, pair_index]
        chosen = hot_blocks[source_tile, selection[target_tile, source_tile]]
        src_start = (source_tile * tile_rows + chosen * BLK).astype(jnp.int32)
        source = lax.dynamic_slice_in_dim(rounded, src_start, BLK, 0)
        ham_block = lax.dynamic_index_in_dim(ham_wide, (target_tile * NHB + block_id).astype(jnp.int32), 0, keepdims=False)
        product = jnp.dot(ham_block, source, preferred_element_type=jnp.float32)
        is_live = (pair_index < pair_counts[target_tile]).astype(jnp.float32)
        row_start = (target_tile * tile_rows + target_block * BLK).astype(jnp.int32)
        current = lax.dynamic_slice_in_dim(accumulated, row_start, BLK, 0)
        return lax.dynamic_update_slice_in_dim(accumulated, current + is_live * product, row_start, 0)

    one_side = lax.fori_loop(0, NTILE * NPAIR, update, jnp.zeros((N, N), jnp.float32))
    return one_side + one_side.T + (diagonal[:, None] + diagonal[None, :]) * iterate


def reference(start_vector, ham_blocks, diagonal, pair_lists, pair_counts, hot_blocks, selection):
    first_iterate = (operator(start_vector, ham_blocks, diagonal, pair_lists, pair_counts, hot_blocks, selection) - center * start_vector) / half_width
    second_iterate = 2.0 * (operator(first_iterate, ham_blocks, diagonal, pair_lists, pair_counts, hot_blocks, selection) - center * first_iterate) / half_width - start_vector
    return first_iterate, second_iterate
```

```python
import jax
import jax.numpy as jnp
from jax import lax
from jax.experimental import pallas as pl
from jax.experimental.pallas import tpu as pltpu
from jax.sharding import Mesh, PartitionSpec as P
import numpy as np

center = 0.25
scale = 1.0 / 2.5
axes = ("zl", "x", "zh", "y", "k")
sizes = (4, 4, 2, 4, 2)
B = 128
T = 768
R = 256
bf16 = jnp.bfloat16
f32 = jnp.float32


def permute(value, target):
    places = list(np.ndindex(*sizes))
    pairs = [
        (int(np.ravel_multi_index(p, sizes)), int(np.ravel_multi_index(target(*p), sizes)))
        for p in places
    ]
    return lax.ppermute(value, axes, pairs)


def z_xor(n):
    return lambda zl, x, zh, y, k: (zl ^ n, x, zh, y, k)


def y_shift(n):
    return lambda zl, x, zh, y, k: (zl, x, zh, (y + n) % 4, k)


def zh_flip(zl, x, zh, y, k):
    return (zl, x, 1 - zh, y, k)


def k_flip(zl, x, zh, y, k):
    return (zl, x, zh, y, 1 - k)


def mirror(zl, x, zh, y, k):
    r, c = zl * 4 + x, zh * 8 + y * 2 + k
    return (c // 4, c % 4, r // 8, (r % 8) // 2, r % 2)


def barrier(*values):
    return lax.optimization_barrier(values)


def start(block):
    return pl.multiple_of(block * B, B)


def call(kernel, scalars, grid, in_specs, out_specs, out_shape, args, scratch=(), flops=0, moved=0):
    return pl.pallas_call(
        kernel,
        grid_spec=pltpu.PrefetchScalarGridSpec(
            num_scalar_prefetch=len(scalars),
            grid=grid,
            in_specs=in_specs,
            out_specs=out_specs,
            scratch_shapes=list(scratch),
        ),
        out_shape=out_shape,
        cost_estimate=pl.CostEstimate(flops=flops, bytes_accessed=moved, transcendentals=0),
    )(*scalars, *args)


def shape(dims, kind=bf16):
    return jax.ShapeDtypeStruct(dims, kind)


pack_shapes = (shape((2, B, T)), shape((2, T, B)), shape((4, B, T)))


def pack_kernel(ids, hot, sel, x_ref, row_ref, col_ref, near_ref):
    r, c = ids[0], ids[1]
    for h in range(2):
        row_ref[h] = x_ref[pl.ds(start(hot[r, h]), B), :].astype(bf16)
        col_ref[h] = x_ref[:, pl.ds(start(hot[c, h]), B)].astype(bf16)
    for j in range(4):
        block = hot[r, sel[(r // 4) * 4 + j, r]]
        near_ref[j] = x_ref[pl.ds(start(block), B), :].astype(bf16)


def pack(ids, hot, sel, value):
    def whole(dims):
        return pl.BlockSpec(dims, lambda i, *_: (0,) * len(dims))

    return call(
        pack_kernel,
        (ids, hot, sel),
        (1,),
        [whole((T, T))],
        [whole((2, B, T)), whole((2, T, B)), whole((4, B, T))],
        pack_shapes,
        (value,),
        moved=5 << 20,
    )


def choose(ids, sel, slabs, steps):
    def kernel(ids, sel, *refs):
        for n in range(len(slabs)):
            refs[-1][n] = refs[n][0]

    def reader(step):
        def index(j, ids, sel):
            zl, x = ids[0] // 4, ids[0] % 4
            return (sel[zl * 4 + j, (zl ^ step) * 4 + x], 0, 0)

        return pl.BlockSpec((1, B, T), index)

    count = len(slabs)
    return call(
        kernel,
        (ids, sel),
        (4,),
        [reader(step) for step in steps],
        pl.BlockSpec((count, B, T), lambda j, *_: (j, 0, 0)),
        shape((4 * count, B, T)),
        slabs,
        moved=count << 21,
    )


def over_x(payload):
    return lax.all_to_all(payload, "x", 0, 0, tiled=True)


def dense_kernel(mirrored):
    def kernel(ids, lists, counts, ham_ref, out_ref, total):
        r, c = ids[0], ids[1]
        tile = c if mirrored else r
        zl = r // 4

        def clear(i, carry):
            total[i] = jnp.zeros((B, B), f32)
            return carry

        lax.fori_loop(0, 96, clear, 0)

        def add(slot, carry):
            q = lists[0, tile, slot]
            t = lists[1, tile, slot]
            b = lists[2, tile, slot]
            if mirrored:
                zh, y, k = c // 8, (c // 2) % 4, c % 2
                qzh, qy, qk = q // 8, (q // 2) % 4, q % 2
                place = ((qk ^ k) * 4 + ((y - qy + 4) % 4)) * 2 + (qzh ^ zh)
                piece = b // 3
                b = ((piece % 4) * 4 + ((piece // 4) ^ zl)) * 3 + b % 3
            else:
                n, j = (q // 4) ^ zl, q % 4
                place = jnp.where(n < 2, n * 4 + j, 8 + j * 2 + (n - 2))
            at = t * 16 + place
            total[at] = total[at] + ham_ref[b].astype(f32)
            return carry

        lax.fori_loop(0, counts[tile], add, 0)
        for t in range(6):
            for place in range(16):
                block = total[t * 16 + place].astype(bf16)
                if mirrored:
                    out_ref[place * B : (place + 1) * B, t * B : (t + 1) * B] = block
                else:
                    out_ref[t * B : (t + 1) * B, place * B : (place + 1) * B] = block

    return kernel


def dense(ids, lists, counts, hams, mirrored):
    dims = (2048, T) if mirrored else (T, 2048)
    return call(
        dense_kernel(mirrored),
        (ids, lists, counts),
        (1,),
        [pl.BlockSpec((48, B, B), lambda i, *_: (0, 0, 0))],
        pl.BlockSpec(dims, lambda i, *_: (0, 0)),
        shape(dims),
        (hams,),
        scratch=[pltpu.VMEM((96, B, B), f32)],
        flops=1 << 22,
        moved=5 << 20,
    )


def first_products_kernel(ids, sel, ham_t_ref, ham_ref, near_ref, next_ref, *refs):
    slabs, out_ref, wide = refs[:8], refs[8], refs[9]
    c = ids[1]
    zh, y, k = c // 8, (c // 2) % 4, c % 2
    for place in range(16):
        m, flip = place // 2, place % 2
        q = (zh ^ flip) * 8 + ((y - m % 4 + 4) % 4) * 2 + (k ^ (m // 4))
        wide[:, place * B : (place + 1) * B] = slabs[m][flip * 2 + sel[c, q]]
    out_ref[...] = (
        jnp.dot(wide[...], ham_t_ref[...], preferred_element_type=f32)
        + jnp.dot(ham_ref[:, :512], near_ref[...], preferred_element_type=f32)
        + jnp.dot(ham_ref[:, 512:], next_ref[...], preferred_element_type=f32)
    )


def first_products(ids, sel, ham_t, ham, near, following, slabs):
    return call(
        first_products_kernel,
        (ids, sel),
        (T // R,),
        [
            pl.BlockSpec((2048, T), lambda i, *_: (0, 0)),
            pl.BlockSpec((R, 1024), lambda i, *_: (i, 0)),
            pl.BlockSpec((512, T), lambda i, *_: (0, 0)),
            pl.BlockSpec((512, T), lambda i, *_: (0, 0)),
        ]
        + [pl.BlockSpec((4, R, B), lambda i, *_: (0, i, 0))] * 8,
        pl.BlockSpec((R, T), lambda i, *_: (i, 0)),
        shape((T, T), f32),
        (ham_t, ham, near, following, *slabs),
        scratch=[pltpu.VMEM((R, 2048), bf16)],
        flops=2 * T * T * 3072,
        moved=18 << 20,
    )


def finish_kernel(second):
    def kernel(ids, hot, sel, part_ref, ham_ref, far_ref, x_ref, dr_ref, dc_ref, *refs):
        total = part_ref[...] + jnp.dot(ham_ref[...], far_ref[...], preferred_element_type=f32)
        value = x_ref[...]
        applied = total + (dr_ref[...] + dc_ref[...]) * value
        stepped = (applied - center * value) * scale
        if second:
            refs[1][...] = 2.0 * stepped - refs[0][...]
            return
        out_ref, row_ref, col_ref, near_ref = refs
        out_ref[...] = stepped
        i, r, c = pl.program_id(0), ids[0], ids[1]
        for h in range(2):
            col_ref[h] = out_ref[:, pl.ds(start(hot[c, h]), B)].astype(bf16)
            block = hot[r, h]

            @pl.when(block // 2 == i)
            def _(h=h, block=block):
                row_ref[h] = out_ref[pl.ds(start(block % 2), B), :].astype(bf16)

        for j in range(4):
            block = hot[r, sel[(r // 4) * 4 + j, r]]

            @pl.when(block // 2 == i)
            def _(j=j, block=block):
                near_ref[j] = out_ref[pl.ds(start(block % 2), B), :].astype(bf16)

    return kernel


def finish(ids, hot, sel, part, ham, far, value, dr, dc, before=None):
    second = before is not None
    rows = pl.BlockSpec((R, T), lambda i, *_: (i, 0))
    in_specs = [
        rows,
        pl.BlockSpec((R, 1024), lambda i, *_: (i, 1)),
        pl.BlockSpec((1024, T), lambda i, *_: (0, 0)),
        rows,
        pl.BlockSpec((R, 1), lambda i, *_: (i, 0)),
        pl.BlockSpec((1, T), lambda i, *_: (0, 0)),
    ]
    args = (part, ham, far, value, dr, dc)
    if second:
        in_specs, args = in_specs + [rows], args + (before,)
        out_specs, out_shape = rows, shape((T, T), f32)
    else:
        out_specs = [
            rows,
            pl.BlockSpec((2, B, T), lambda i, *_: (0, 0, 0)),
            pl.BlockSpec((2, R, B), lambda i, *_: (0, i, 0)),
            pl.BlockSpec((4, B, T), lambda i, *_: (0, 0, 0)),
        ]
        out_shape = (shape((T, T), f32),) + pack_shapes
    return call(
        finish_kernel(second),
        (ids, hot, sel),
        (T // R,),
        in_specs,
        out_specs,
        out_shape,
        args,
        flops=2 * T * T * 1024,
        moved=12 << 20,
    )


def body(start_vector, ham_blocks, diagonal, lists, counts, hot, sel):
    row_index = lax.axis_index("zl") * 4 + lax.axis_index("x")
    col_index = (lax.axis_index("zh") * 4 + lax.axis_index("y")) * 2 + lax.axis_index("k")
    ids = jnp.stack([row_index, col_index]).astype(jnp.int32)
    dr = lax.dynamic_slice_in_dim(diagonal, row_index * T, T).reshape(T, 1)
    dc = lax.dynamic_slice_in_dim(diagonal, col_index * T, T).reshape(1, T)

    piece = lax.dynamic_slice_in_dim(ham_blocks, col_index * 3, 3).transpose(0, 2, 1)
    piece = permute(piece, mirror)
    row, col, near_out = pack(ids, hot, sel, start_vector)
    ham = dense(ids, lists, counts, ham_blocks, False)

    ham_t = None
    outs = []
    value, before = start_vector, None
    for step in range(2):
        row, col, near_out, piece = barrier(row, col, near_out, piece)
        z1 = permute(row, z_xor(1))
        zh = permute(col, zh_flip)
        near = over_x(near_out)
        pieces = [permute(piece, z_xor(n)) for n in (1, 2, 3)] if step == 0 else []
        row, col, z1, zh, near, *pieces = barrier(row, col, z1, zh, near, *pieces)
        both = jnp.concatenate([col, zh])
        z2 = permute(row, z_xor(2))
        z3 = permute(row, z_xor(3))
        ys = [permute(both, y_shift(n)) for n in (1, 2, 3)]
        following = over_x(choose(ids, sel, (z1,), (1,)))
        extra = []
        if step == 0:
            joined = jnp.stack([piece] + pieces)
            extra = [over_x(jnp.broadcast_to(joined[None], (4, 4, 3, B, B)).reshape(48, B, B))]
        z2, z3, following, both, *rest = barrier(z2, z3, following, both, *ys, *extra)
        mine = [both] + rest[:3]
        others = [permute(m, k_flip) for m in mine]
        far = over_x(choose(ids, sel, (z2, z3), (2, 3)))
        if step == 0:
            ham_t = dense(ids, lists, counts, rest[3], True)
        part = first_products(
            ids, sel, ham_t, ham, near.reshape(512, T), following.reshape(512, T), mine + others
        )
        far = far.reshape(1024, T)
        if step == 0:
            value, row, col, near_out = finish(ids, hot, sel, part, ham, far, value, dr, dc)
            outs.append(value)
        else:
            outs.append(finish(ids, hot, sel, part, ham, far, value, dr, dc, start_vector))
    return tuple(outs)


def solution(mesh):
    fine = Mesh(mesh.devices.reshape(sizes), axes)
    rows, cols = ("zl", "x"), ("zh", "y", "k")
    in_specs = (P(rows, cols), P(rows, None, None), P(), P(), P(), P(), P())
    out_specs = (P(rows, cols), P(rows, cols))
    return jax.shard_map(body, mesh=fine, in_specs=in_specs, out_specs=out_specs, check_vma=False)
```

```python
import jax
import jax.numpy as jnp
from jax import lax
from jax.experimental import pallas as pl
from jax.experimental.pallas import tpu as pltpu
from jax.sharding import Mesh, PartitionSpec as P
import numpy as np

center = 0.25
scale = 1.0 / 2.5
axes = ("zl", "x", "zh", "y", "k")
sizes = (4, 4, 2, 4, 2)
B = 128
T = 768
R = 256
bf16 = jnp.bfloat16
f32 = jnp.float32


def permute(value, target):
    places = list(np.ndindex(*sizes))
    pairs = [
        (int(np.ravel_multi_index(p, sizes)), int(np.ravel_multi_index(target(*p), sizes)))
        for p in places
    ]
    return lax.ppermute(value, axes, pairs)


def z_xor(n):
    return lambda zl, x, zh, y, k: (zl ^ n, x, zh, y, k)


def x_shift(n):
    return lambda zl, x, zh, y, k: (zl, (x + n) % 4, zh, y, k)


def zh_flip(zl, x, zh, y, k):
    return (zl, x, 1 - zh, y, k)


def mirror(zl, x, zh, y, k):
    r, c = zl * 4 + x, zh * 8 + y * 2 + k
    return (c // 4, c % 4, r // 8, (r % 8) // 2, r % 2)


def barrier(*values):
    return lax.optimization_barrier(values)


def start(block):
    return pl.multiple_of(block * B, B)


def call(kernel, scalars, grid, in_specs, out_specs, out_shape, args, scratch=(), flops=0, moved=0, room=1):
    return pl.pallas_call(
        kernel,
        grid_spec=pltpu.PrefetchScalarGridSpec(
            num_scalar_prefetch=len(scalars),
            grid=grid,
            in_specs=in_specs,
            out_specs=out_specs,
            scratch_shapes=list(scratch),
        ),
        out_shape=out_shape,
        compiler_params=pltpu.CompilerParams(vmem_limit_bytes=room << 20),
        cost_estimate=pl.CostEstimate(flops=flops, bytes_accessed=moved, transcendentals=0),
    )(*scalars, *args)


def shape(dims, kind=bf16):
    return jax.ShapeDtypeStruct(dims, kind)


pack_shapes = (shape((2, B, T)), shape((2, T, B)))


def pack_kernel(ids, hot, x_ref, row_ref, col_ref):
    r, c = ids[0], ids[1]
    for h in range(2):
        row_ref[h] = x_ref[pl.ds(start(hot[r, h]), B), :].astype(bf16)
        col_ref[h] = x_ref[:, pl.ds(start(hot[c, h]), B)].astype(bf16)

def pack(ids, hot, value):
    def whole(dims):
        return pl.BlockSpec(dims, lambda i, *_: (0,) * len(dims))

    return call(
        pack_kernel,
        (ids, hot),
        (1,),
        [whole((T, T))],
        [whole((2, B, T)), whole((2, T, B))],
        pack_shapes,
        (value,),
        moved=5 << 20,
        room=16,
    )


anywhere = pl.BlockSpec(memory_space=pl.ANY)


def copy_all(pairs, done):
    copies = [
        pltpu.make_async_copy(source, target, done.at[i])
        for i, (source, target) in enumerate(pairs)
    ]
    for copy in copies:
        copy.start()
    for copy in copies:
        copy.wait()


def over_x(ids, sel, slabs, step):
    def kernel(ids, sel, slabs_ref, *refs):
        zl, x = ids[0] // 4, ids[0] % 4
        q = (zl ^ step) * 4 + x
        copy_all(
            [(slabs_ref.at[sel[zl * 4 + (x + n) % 4, q]], refs[n].at[0]) for n in range(4)],
            refs[4],
        )

    chosen = call(
        kernel,
        (ids, sel),
        (1,),
        [anywhere],
        [anywhere] * 4,
        [shape((1, B, T))] * 4,
        (slabs,),
        scratch=[pltpu.SemaphoreType.DMA((4,))],
        moved=256 << 20,
    )
    return [chosen[0]] + [permute(chosen[n], x_shift(n)) for n in (1, 2, 3)]


def over_yk(ids, sel, slabs, flip):
    def kernel(ids, sel, slabs_ref, out_ref, done):
        zh, q = ids[1] // 8, ids[1] ^ (8 * flip)
        copy_all(
            [(slabs_ref.at[sel[zh * 8 + i, q]], out_ref.at[i]) for i in range(8)], done
        )

    chosen = call(
        kernel,
        (ids, sel),
        (1,),
        [anywhere],
        anywhere,
        shape((8, T, B)),
        (slabs,),
        scratch=[pltpu.SemaphoreType.DMA((8,))],
        moved=256 << 20,
    )
    return lax.all_to_all(chosen, ("y", "k"), 0, 0, tiled=True)


def dense_kernel(mirrored):
    def kernel(ids, lists, counts, ham_ref, out_ref, total):
        r, c = ids[0], ids[1]
        tile = c if mirrored else r
        zl = r // 4

        def clear(i, carry):
            total[i] = jnp.zeros((B, B), f32)
            return carry

        lax.fori_loop(0, 96, clear, 0)

        def add(slot, carry):
            q = lists[0, tile, slot]
            t = lists[1, tile, slot]
            b = lists[2, tile, slot]
            if mirrored:
                place = q ^ (c // 8 * 8)
                piece = b // 3
                b = ((piece % 4) * 4 + ((piece // 4) ^ zl)) * 3 + b % 3
            else:
                place = ((q // 4) ^ zl) * 4 + (r + 4 - q % 4) % 4
            at = t * 16 + place
            total[at] = total[at] + ham_ref[b].astype(f32)
            return carry

        lax.fori_loop(0, counts[tile], add, 0)
        for t in range(6):
            for place in range(16):
                block = total[t * 16 + place].astype(bf16)
                if mirrored:
                    out_ref[place * B : (place + 1) * B, t * B : (t + 1) * B] = block
                else:
                    out_ref[t * B : (t + 1) * B, place * B : (place + 1) * B] = block

    return kernel


def dense(ids, lists, counts, hams, mirrored):
    dims = (2048, T) if mirrored else (T, 2048)
    return call(
        dense_kernel(mirrored),
        (ids, lists, counts),
        (1,),
        [pl.BlockSpec((48, B, B), lambda i, *_: (0, 0, 0))],
        pl.BlockSpec(dims, lambda i, *_: (0, 0)),
        shape(dims),
        (hams,),
        scratch=[pltpu.VMEM((96, B, B), f32)],
        flops=1 << 22,
        moved=5 << 20,
        room=28,
    )


def first_products_kernel(second):
    def kernel(ham_t_ref, ham_ref, x_ref, dr_ref, dc_ref, yk0_ref, yk1_ref, *refs):
        slabs, out_ref, wide = refs[:8], refs[-2], refs[-1]
        for i in range(8):
            wide[:, i * B : (i + 1) * B] = yk0_ref[i]
            wide[:, (8 + i) * B : (9 + i) * B] = yk1_ref[i]
        stacked = jnp.concatenate([slab[0] for slab in slabs], axis=0)
        total = jnp.dot(wide[...], ham_t_ref[...], preferred_element_type=f32) + jnp.dot(
            ham_ref[...], stacked, preferred_element_type=f32
        )
        total = total + (dr_ref[...] + dc_ref[...] - center) * x_ref[...]
        if second:
            total = total - refs[8][...] * (0.5 / scale)
        out_ref[...] = total

    return kernel


rows = pl.BlockSpec((R, T), lambda i, *_: (i, 0))
slab = pl.BlockSpec((1, B, T), lambda i, *_: (0, 0, 0))


def first_products(ham_t, ham, value, dr, dc, yk0, yk1, slabs, before=None):
    extra = () if before is None else (before,)
    return call(
        first_products_kernel(before is not None),
        (),
        (T // R,),
        [
            pl.BlockSpec((2048, T), lambda i, *_: (0, 0)),
            pl.BlockSpec((R, 1024), lambda i, *_: (i, 0)),
            rows,
            pl.BlockSpec((R, 1), lambda i, *_: (i, 0)),
            pl.BlockSpec((1, T), lambda i, *_: (0, 0)),
        ]
        + [pl.BlockSpec((8, R, B), lambda i, *_: (0, i, 0))] * 2
        + [slab] * 8
        + [rows] * len(extra),
        rows,
        shape((T, T), f32),
        (ham_t, ham, value, dr, dc, yk0, yk1, *slabs, *extra),
        scratch=[pltpu.VMEM((R, 2048), bf16)],
        flops=2 * T * T * 3072,
        moved=18 << 20,
        room=32,
    )


def finish_kernel(second):
    def kernel(ids, hot, part_ref, ham_ref, *refs):
        stacked = jnp.concatenate([ref[0] for ref in refs[:8]], axis=0)
        out_ref = refs[8]
        total = part_ref[...] + jnp.dot(ham_ref[...], stacked, preferred_element_type=f32)
        if second:
            out_ref[...] = total * (2.0 * scale)
            return
        row_ref, col_ref = refs[9:]
        out_ref[...] = total * scale
        i, r, c = pl.program_id(0), ids[0], ids[1]
        for h in range(2):
            col_ref[h] = out_ref[:, pl.ds(start(hot[c, h]), B)].astype(bf16)
            block = hot[r, h]

            @pl.when(block // 2 == i)
            def _(h=h, block=block):
                row_ref[h] = out_ref[pl.ds(start(block % 2), B), :].astype(bf16)

    return kernel


def finish(ids, hot, part, ham, slabs, second):
    out_specs, out_shape = rows, shape((T, T), f32)
    if not second:
        out_specs = [
            rows,
            pl.BlockSpec((2, B, T), lambda i, *_: (0, 0, 0)),
            pl.BlockSpec((2, R, B), lambda i, *_: (0, i, 0)),
        ]
        out_shape = (out_shape,) + pack_shapes
    return call(
        finish_kernel(second),
        (ids, hot),
        (T // R,),
        [rows, pl.BlockSpec((R, 1024), lambda i, *_: (i, 1))] + [slab] * 8,
        out_specs,
        out_shape,
        (part, ham, *slabs),
        flops=2 * T * T * 1024,
        moved=8 << 20,
        room=24,
    )


def spread(pieces):
    count = len(pieces)

    def kernel(*refs):
        out_ref = refs[count]
        copy_all(
            [(refs[n], out_ref.at[j, n]) for j in range(4) for n in range(count)], refs[-1]
        )

    return call(
        kernel,
        (),
        (1,),
        [anywhere] * count,
        anywhere,
        shape((4, count) + pieces[0].shape),
        pieces,
        scratch=[pltpu.SemaphoreType.DMA((4 * count,))],
        moved=256 << 20,
    )


def body(start_vector, ham_blocks, diagonal, lists, counts, hot, sel):
    row_index = lax.axis_index("zl") * 4 + lax.axis_index("x")
    col_index = (lax.axis_index("zh") * 4 + lax.axis_index("y")) * 2 + lax.axis_index("k")
    ids = jnp.stack([row_index, col_index]).astype(jnp.int32)
    dr = lax.dynamic_slice_in_dim(diagonal, row_index * T, T).reshape(T, 1)
    dc = lax.dynamic_slice_in_dim(diagonal, col_index * T, T).reshape(1, T)

    piece = lax.dynamic_slice_in_dim(ham_blocks, col_index * 3, 3).transpose(0, 2, 1)
    piece = permute(piece, mirror)
    row, col = pack(ids, hot, start_vector)
    ham_t = ham = None
    outs = []
    value = start_vector
    for step in range(2):
        first = step == 0
        row, col, piece = barrier(row, col, piece)
        z1 = permute(row, z_xor(1))
        zh = permute(col, zh_flip)
        pieces = [permute(piece, z_xor(n)) for n in (1, 2, 3)] if first else []
        x0 = over_x(ids, sel, row, 0)
        yk0 = over_yk(ids, sel, col, 0)
        if first:
            ham = dense(ids, lists, counts, ham_blocks, False)
        row, z1, zh, x0, yk0, ham, dr, dc, pieces = barrier(
            row, z1, zh, x0, yk0, ham, dr, dc, pieces
        )
        z2 = permute(row, z_xor(2))
        x1 = over_x(ids, sel, z1, 1)
        if first:
            hams = spread([piece] + pieces).reshape(48, B, B)
            hams = lax.all_to_all(hams, "x", 0, 0, tiled=True)
            row, zh, z2, x1, hams = barrier(row, zh, z2, x1, hams)
        else:
            yk1 = over_yk(ids, sel, zh, 1)
            row, z2, x1, yk1 = barrier(row, z2, x1, yk1)
        z3 = permute(row, z_xor(3))
        x2 = over_x(ids, sel, z2, 2)
        if first:
            yk1 = over_yk(ids, sel, zh, 1)
            ham_t = dense(ids, lists, counts, hams, True)
            z3, x2, yk1, ham_t = barrier(z3, x2, yk1, ham_t)
            part = first_products(ham_t, ham, value, dr, dc, yk0, yk1, x0 + x1)
        else:
            part = first_products(ham_t, ham, value, dr, dc, yk0, yk1, x0 + x1, start_vector)
            z3, x2, part = barrier(z3, x2, part)
        x3 = over_x(ids, sel, z3, 3)
        result = finish(ids, hot, part, ham, x2 + x3, not first)
        if first:
            value, row, col = result
            result = value
        outs.append(result)
    return tuple(outs)


def solution(mesh):
    fine = Mesh(mesh.devices.reshape(sizes), axes)
    rows, cols = ("zl", "x"), ("zh", "y", "k")
    in_specs = (P(rows, cols), P(rows, None, None), P(), P(), P(), P(), P())
    out_specs = (P(rows, cols), P(rows, cols))
    return jax.shard_map(body, mesh=fine, in_specs=in_specs, out_specs=out_specs, check_vma=False)
```

```python
import jax
import jax.numpy as jnp
from jax import lax
from jax.experimental import pallas as pl
from jax.experimental.pallas import tpu as pltpu
from jax.sharding import Mesh, PartitionSpec as P
import numpy as np

center = 0.25
scale = 1.0 / 2.5
axes = ("zl", "x", "zh", "y", "k")
sizes = (4, 4, 2, 4, 2)
B = 128
T = 768
R = 256
bf16 = jnp.bfloat16
f32 = jnp.float32


def permute(value, target):
    places = list(np.ndindex(*sizes))
    pairs = [
        (int(np.ravel_multi_index(p, sizes)), int(np.ravel_multi_index(target(*p), sizes)))
        for p in places
    ]
    return lax.ppermute(value, axes, pairs)


def z_xor(n):
    return lambda zl, x, zh, y, k: (zl ^ n, x, zh, y, k)


def x_shift(n):
    return lambda zl, x, zh, y, k: (zl, (x + n) % 4, zh, y, k)


def zh_flip(zl, x, zh, y, k):
    return (zl, x, 1 - zh, y, k)


def mirror(zl, x, zh, y, k):
    r, c = zl * 4 + x, zh * 8 + y * 2 + k
    return (c // 4, c % 4, r // 8, (r % 8) // 2, r % 2)


def barrier(*values):
    return lax.optimization_barrier(values)


def start(block):
    return pl.multiple_of(block * B, B)


def call(kernel, scalars, grid, in_specs, out_specs, out_shape, args, scratch=(), flops=0, moved=0, room=1, pinned=False):
    return pl.pallas_call(
        kernel,
        grid_spec=pltpu.PrefetchScalarGridSpec(
            num_scalar_prefetch=len(scalars),
            grid=grid,
            in_specs=in_specs,
            out_specs=out_specs,
            scratch_shapes=list(scratch),
        ),
        out_shape=out_shape,
        compiler_params=pltpu.CompilerParams(vmem_limit_bytes=room << 20),
        cost_estimate=pl.CostEstimate(flops=flops, bytes_accessed=moved, transcendentals=0),
    )(*scalars, *(pltpu.with_memory_space_constraint(arg, pltpu.HBM) if pinned else arg for arg in args))


def shape(dims, kind=bf16):
    return pltpu.HBM(dims, kind)


def free_shape(dims, kind=bf16):
    return jax.ShapeDtypeStruct(dims, kind)


def whole(dims):
    return pl.BlockSpec(dims, lambda i, *_: (0,) * len(dims))


send_shapes = (
    [shape((2, B, T)), shape((2, T, B))] + [shape((1, B, T))] * 4 + [shape((8, T, B))]
)


def choose_rows(ids, sel, step, slabs_ref, refs):
    zl, x = ids[0] // 4, ids[0] % 4
    for n in range(4):
        refs[n][0] = slabs_ref[sel[zl * 4 + (x + n) % 4, (zl ^ step) * 4 + x]]


def choose_cols(ids, sel, flip, slabs_ref, out_ref, stride=1, offset=0):
    zh, q = ids[1] // 8, ids[1] ^ (8 * flip)
    for i in range(8):
        out_ref[i * stride + offset] = slabs_ref[sel[zh * 8 + i, q]]


def pack_kernel(ids, hot, sel, x_ref, row_ref, col_ref, *refs):
    r, c = ids[0], ids[1]
    for h in range(2):
        row_ref[h] = x_ref[pl.ds(start(hot[r, h]), B), :].astype(bf16)
        col_ref[h] = x_ref[:, pl.ds(start(hot[c, h]), B)].astype(bf16)
    choose_rows(ids, sel, 0, row_ref, refs[:4])
    choose_cols(ids, sel, 0, col_ref, refs[4])


def pack(ids, hot, sel, value):
    return call(
        pack_kernel,
        (ids, hot, sel),
        (1,),
        [whole((T, T))],
        [whole(s.shape) for s in send_shapes],
        send_shapes,
        (value,),
        moved=5 << 20,
        room=32,
    )


def next_slabs(ids, sel, rows, step, *cols):
    def kernel(ids, sel, *refs):
        outs = refs[1 + len(cols) :]
        choose_rows(ids, sel, step, refs[0], outs[:4])
        if len(cols) == 1:
            choose_cols(ids, sel, 1, refs[1], outs[4])
        if len(cols) == 2:
            choose_cols(ids, sel, 0, refs[1], outs[4], 2, 0)
            choose_cols(ids, sel, 1, refs[2], outs[4], 2, 1)

    out_shapes = send_shapes[2:6] + [shape((8 * len(cols), T, B))] * (len(cols) > 0)
    args = (rows, *cols)
    return call(
        kernel,
        (ids, sel),
        (1,),
        [whole(arg.shape) for arg in args],
        [whole(s.shape) for s in out_shapes],
        out_shapes,
        args,
        moved=4 << 20,
        room=32,
    )


def over_x(chosen):
    return [chosen[0]] + [permute(chosen[n], x_shift(n)) for n in (1, 2, 3)]


def over_yk(chosen):
    return lax.all_to_all(chosen, ("y", "k"), 0, 0, tiled=True)


def dense_kernel(mirrored):
    def kernel(ids, lists, counts, ham_ref, out_ref, total):
        r, c = ids[0], ids[1]
        tile = c if mirrored else r
        zl = r // 4

        def clear(i, carry):
            total[i] = jnp.zeros((B, B), f32)
            return carry

        lax.fori_loop(0, 96, clear, 0)

        def add(slot, carry):
            q = lists[0, tile, slot]
            t = lists[1, tile, slot]
            b = lists[2, tile, slot]
            if mirrored:
                place = q ^ (c // 8 * 8)
                piece = b // 3
                b = ((piece % 4) * 4 + ((piece // 4) ^ zl)) * 3 + b % 3
            else:
                place = ((q // 4) ^ zl) * 4 + (r + 4 - q % 4) % 4
            at = t * 16 + place
            total[at] = total[at] + ham_ref[b].astype(f32)
            return carry

        lax.fori_loop(0, counts[tile], add, 0)
        for t in range(6):
            for place in range(16):
                block = total[t * 16 + place].astype(bf16)
                if mirrored:
                    out_ref[place * B : (place + 1) * B, t * B : (t + 1) * B] = block
                else:
                    out_ref[t * B : (t + 1) * B, place * B : (place + 1) * B] = block

    return kernel


def dense(ids, lists, counts, hams, mirrored):
    dims = (2048, T) if mirrored else (T, 2048)
    return call(
        dense_kernel(mirrored),
        (ids, lists, counts),
        (1,),
        [pl.BlockSpec((48, B, B), lambda i, *_: (0, 0, 0))],
        pl.BlockSpec(dims, lambda i, *_: (0, 0)),
        shape(dims),
        (hams,),
        scratch=[pltpu.VMEM((96, B, B), f32)],
        flops=1 << 22,
        moved=5 << 20,
        room=28,
    )


def first_products_kernel(second, arrays):
    def kernel(ham_t_ref, ham_ref, x_ref, dr_ref, dc_ref, *refs):
        slabs, out_ref, wide = refs[:8], refs[-2], refs[-1]
        yk = refs[8 : 8 + arrays]
        for i in range(8):
            wide[:, i * B : (i + 1) * B] = yk[0][i] if arrays == 2 else yk[0][2 * i]
            wide[:, (8 + i) * B : (9 + i) * B] = yk[1][i] if arrays == 2 else yk[0][2 * i + 1]
        stacked = jnp.concatenate([slab[0] for slab in slabs], axis=0)
        total = jnp.dot(wide[...], ham_t_ref[...], preferred_element_type=f32) + jnp.dot(
            ham_ref[...], stacked, preferred_element_type=f32
        )
        total = total + (dr_ref[...] + dc_ref[...] - center) * x_ref[...]
        if second:
            total = total - refs[8 + arrays][...] * (0.5 / scale)
        out_ref[...] = total

    return kernel


rows = pl.BlockSpec((R, T), lambda i, *_: (i, 0))
slab = pl.BlockSpec((1, B, T), lambda i, *_: (0, 0, 0))


def first_products(ham_t, ham, value, dr, dc, yk, slabs, before=None):
    extra = () if before is None else (before,)
    return call(
        first_products_kernel(before is not None, len(yk)),
        (),
        (T // R,),
        [
            pl.BlockSpec((2048, T), lambda i, *_: (0, 0)),
            pl.BlockSpec((R, 1024), lambda i, *_: (i, 0)),
            rows,
            pl.BlockSpec((R, 1), lambda i, *_: (i, 0)),
            pl.BlockSpec((1, T), lambda i, *_: (0, 0)),
        ]
        + [slab] * 8
        + [pl.BlockSpec((a.shape[0], R, B), lambda i, *_: (0, i, 0)) for a in yk]
        + [rows] * len(extra),
        rows,
        free_shape((T, T), f32),
        (ham_t, ham, value, dr, dc, *slabs, *yk, *extra),
        scratch=[pltpu.VMEM((R, 2048), bf16)],
        flops=2 * T * T * 3072,
        moved=18 << 20,
        room=32,
        pinned=True,
    )


def finish_kernel(second):
    def kernel(ids, hot, sel, part_ref, ham_ref, *refs):
        stacked = jnp.concatenate([ref[0] for ref in refs[:8]], axis=0)
        out_ref = refs[8]
        total = part_ref[...] + jnp.dot(ham_ref[...], stacked, preferred_element_type=f32)
        if second:
            out_ref[...] = total * (2.0 * scale)
            return
        row_ref, col_ref = refs[9:11]
        out_ref[...] = total * scale
        i, r, c = pl.program_id(0), ids[0], ids[1]
        for h in range(2):
            col_ref[h] = out_ref[:, pl.ds(start(hot[c, h]), B)].astype(bf16)
            block = hot[r, h]

            @pl.when(block // 2 == i)
            def _(h=h, block=block):
                row_ref[h] = out_ref[pl.ds(start(block % 2), B), :].astype(bf16)

        @pl.when(i == T // R - 1)
        def _():
            choose_rows(ids, sel, 0, row_ref, refs[11:15])

    return kernel


def finish(ids, hot, sel, part, ham, slabs, second):
    out_specs, out_shape = rows, shape((T, T), f32)
    if not second:
        out_specs = [rows, whole((2, B, T)), pl.BlockSpec((2, R, B), lambda i, *_: (0, i, 0))]
        out_specs += [whole((1, B, T))] * 4
        out_shape = [out_shape] + send_shapes[:6]
    return call(
        finish_kernel(second),
        (ids, hot, sel),
        (T // R,),
        [rows, pl.BlockSpec((R, 1024), lambda i, *_: (i, 1))] + [slab] * 8,
        out_specs,
        out_shape,
        (part, ham, *slabs),
        flops=2 * T * T * 1024,
        moved=8 << 20,
        room=32,
    )


def spread(pieces):
    def kernel(*refs):
        for n in range(4):
            refs[4][0, n] = refs[n][...]

    dims = pieces[0].shape
    return call(
        kernel,
        (),
        (4,),
        [whole(dims)] * 4,
        pl.BlockSpec((1, 4) + dims, lambda i: (i, 0, 0, 0, 0)),
        shape((4, 4) + dims),
        pieces,
        moved=4 << 20,
        room=16,
    )


def body(start_vector, ham_blocks, diagonal, lists, counts, hot, sel):
    row_index = lax.axis_index("zl") * 4 + lax.axis_index("x")
    col_index = (lax.axis_index("zh") * 4 + lax.axis_index("y")) * 2 + lax.axis_index("k")
    ids = jnp.stack([row_index, col_index]).astype(jnp.int32)
    dr = lax.dynamic_slice_in_dim(diagonal, row_index * T, T).reshape(T, 1)
    dc = lax.dynamic_slice_in_dim(diagonal, col_index * T, T).reshape(1, T)

    piece = lax.dynamic_slice_in_dim(ham_blocks, col_index * 3, 3).transpose(0, 2, 1)
    piece = permute(piece, mirror)
    row, col, *sends = pack(ids, hot, sel, start_vector)
    ham_t = ham = None
    outs = []
    value = start_vector
    for step in range(2):
        first = step == 0
        row, col, sends, piece = barrier(row, col, sends, piece)
        z1 = permute(row, z_xor(1))
        zh = permute(col, zh_flip)
        x0 = over_x(sends[:4])
        if first:
            pieces = [piece] + [permute(piece, z_xor(n)) for n in (1, 2, 3)]
            yk0 = over_yk(sends[4])
            sends = next_slabs(ids, sel, z1, 1, zh)
            ham = dense(ids, lists, counts, ham_blocks, False)
            hams = spread(pieces)
            row, sends, x0, yk0, ham, dr, dc, hams = barrier(
                row, sends, x0, yk0, ham, dr, dc, hams
            )
        else:
            sends = next_slabs(ids, sel, z1, 1, col, zh)
            row, sends, x0 = barrier(row, sends, x0)
        z2 = permute(row, z_xor(2))
        x1 = over_x(sends[:4])
        later = sends[4]
        sends = next_slabs(ids, sel, z2, 2)
        if first:
            hams = lax.all_to_all(hams.reshape(48, B, B), "x", 0, 0, tiled=True)
            row, sends, x1, hams, later = barrier(row, sends, x1, hams, later)
            yk = [yk0, over_yk(later)]
        else:
            yk = [over_yk(later)]
            row, sends, x1 = barrier(row, sends, x1)
        z3 = permute(row, z_xor(3))
        x2 = over_x(sends)
        sends = next_slabs(ids, sel, z3, 3)
        if first:
            ham_t = dense(ids, lists, counts, hams, True)
        sends, x2, yk, ham_t = barrier(sends, x2, yk, ham_t)
        x3 = over_x(sends)
        before = () if first else (start_vector,)
        part = first_products(ham_t, ham, value, dr, dc, yk, x0 + x1, *before)
        result = finish(ids, hot, sel, part, ham, x2 + x3, not first)
        if first:
            value, row, col, *sends = result
            result = value
        outs.append(result)
    return tuple(outs)


def solution(mesh):
    fine = Mesh(mesh.devices.reshape(sizes), axes)
    rows, cols = ("zl", "x"), ("zh", "y", "k")
    in_specs = (P(rows, cols), P(rows, None, None), P(), P(), P(), P(), P())
    out_specs = (P(rows, cols), P(rows, cols))
    return jax.shard_map(body, mesh=fine, in_specs=in_specs, out_specs=out_specs, check_vma=False)
```

```python
import jax
import jax.numpy as jnp
from jax import lax
from jax.experimental import pallas as pl
from jax.experimental.pallas import tpu as pltpu
from jax.sharding import Mesh, PartitionSpec as P
import numpy as np

center = 0.25
scale = 1.0 / 2.5
axes = ("zl", "x", "zh", "y", "k")
sizes = (4, 4, 2, 4, 2)
B = 128
T = 768
R = 256
bf16 = jnp.bfloat16
f32 = jnp.float32


def permute(value, target):
    places = list(np.ndindex(*sizes))
    pairs = [
        (int(np.ravel_multi_index(p, sizes)), int(np.ravel_multi_index(target(*p), sizes)))
        for p in places
    ]
    return lax.ppermute(value, axes, pairs)


def z_xor(n):
    return lambda zl, x, zh, y, k: (zl ^ n, x, zh, y, k)


def x_shift(n):
    return lambda zl, x, zh, y, k: (zl, (x + n) % 4, zh, y, k)


def zh_flip(zl, x, zh, y, k):
    return (zl, x, 1 - zh, y, k)


def mirror(zl, x, zh, y, k):
    r, c = zl * 4 + x, zh * 8 + y * 2 + k
    return (c // 4, c % 4, r // 8, (r % 8) // 2, r % 2)


def barrier(*values):
    return lax.optimization_barrier(values)


def start(block):
    return pl.multiple_of(block * B, B)


def call(kernel, scalars, grid, in_specs, out_specs, out_shape, args, scratch=(), flops=0, moved=0, room=1, pinned=False):
    return pl.pallas_call(
        kernel,
        grid_spec=pltpu.PrefetchScalarGridSpec(
            num_scalar_prefetch=len(scalars),
            grid=grid,
            in_specs=in_specs,
            out_specs=out_specs,
            scratch_shapes=list(scratch),
        ),
        out_shape=out_shape,
        compiler_params=pltpu.CompilerParams(vmem_limit_bytes=room << 20),
        cost_estimate=pl.CostEstimate(flops=flops, bytes_accessed=moved, transcendentals=0),
    )(*scalars, *(pltpu.with_memory_space_constraint(arg, pltpu.HBM) if pinned else arg for arg in args))


def shape(dims, kind=bf16):
    return pltpu.HBM(dims, kind)


def free_shape(dims, kind=bf16):
    return jax.ShapeDtypeStruct(dims, kind)


def whole(dims):
    return pl.BlockSpec(dims, lambda i, *_: (0,) * len(dims))


send_shapes = (
    [shape((2, B, T)), shape((2, T, B))] + [shape((1, B, T))] * 4 + [shape((8, T, B))]
)


def choose_rows(ids, sel, step, slabs_ref, refs, at=0):
    zl, x = ids[0] // 4, ids[0] % 4
    for n in range(4):
        refs[n][at] = slabs_ref[sel[zl * 4 + (x + n) % 4, (zl ^ step) * 4 + x]]


def choose_cols(ids, sel, flip, slabs_ref, out_ref):
    zh, q = ids[1] // 8, ids[1] ^ (8 * flip)
    for i in range(8):
        out_ref[i] = slabs_ref[sel[zh * 8 + i, q]]


def pack_kernel(ids, hot, sel, x_ref, row_ref, col_ref, *refs):
    r, c = ids[0], ids[1]
    for h in range(2):
        row_ref[h] = x_ref[pl.ds(start(hot[r, h]), B), :].astype(bf16)
        col_ref[h] = x_ref[:, pl.ds(start(hot[c, h]), B)].astype(bf16)
    choose_rows(ids, sel, 0, row_ref, refs[:4])
    choose_cols(ids, sel, 0, col_ref, refs[4])


def pack(ids, hot, sel, value):
    return call(
        pack_kernel,
        (ids, hot, sel),
        (1,),
        [whole((T, T))],
        [whole(s.shape) for s in send_shapes],
        send_shapes,
        (value,),
        moved=5 << 20,
        room=32,
    )


def next_slabs(ids, sel, rows, steps, cols=None):
    count = len(rows)

    def kernel(ids, sel, *refs):
        outs = refs[count + (cols is not None) :]
        for m in range(count):
            choose_rows(ids, sel, steps[m], refs[m], outs[:4], m)
        if cols is not None:
            choose_cols(ids, sel, 1, refs[count], outs[4])

    out_shapes = [shape((count, B, T))] * 4 + [shape((8, T, B))] * (cols is not None)
    args = rows if cols is None else rows + [cols]
    return call(
        kernel,
        (ids, sel),
        (1,),
        [whole(arg.shape) for arg in args],
        [whole(s.shape) for s in out_shapes],
        out_shapes,
        args,
        moved=4 << 20,
        room=32,
    )


def over_x(chosen):
    return [chosen[0]] + [permute(chosen[n], x_shift(n)) for n in (1, 2, 3)]


def over_yk(chosen):
    return lax.all_to_all(chosen, ("y", "k"), 0, 0, tiled=True)


def dense_kernel(mirrored):
    def kernel(ids, lists, counts, *refs):
        out_ref, held, total = refs[-3:]
        ham_ref = refs[0]
        r, c = ids[0], ids[1]
        tile = c if mirrored else r
        if mirrored:
            ham_ref = held
            for n in range(4):
                ham_ref[n * 12 : (n + 1) * 12] = refs[n][...]

        def clear(i, carry):
            total[i] = jnp.zeros((B, B), f32)
            return carry

        lax.fori_loop(0, 96, clear, 0)

        def add(slot, carry):
            q = lists[0, tile, slot]
            t = lists[1, tile, slot]
            b = lists[2, tile, slot]
            if mirrored:
                place = q ^ (c // 8 * 8)
                piece = b // 3
                b = ((r + 4 - piece % 4) % 4 * 4 + ((piece // 4) ^ (r // 4))) * 3 + b % 3
            else:
                place = ((q // 4) ^ (r // 4)) * 4 + (r + 4 - q % 4) % 4
            at = t * 16 + place
            total[at] = total[at] + ham_ref[b].astype(f32)
            return carry

        lax.fori_loop(0, counts[tile], add, 0)
        for t in range(6):
            for place in range(16):
                block = total[t * 16 + place].astype(bf16)
                if mirrored:
                    out_ref[place * B : (place + 1) * B, t * B : (t + 1) * B] = block
                else:
                    out_ref[t * B : (t + 1) * B, place * B : (place + 1) * B] = block

    return kernel


def dense(ids, lists, counts, hams, mirrored):
    dims = (2048, T) if mirrored else (T, 2048)
    return call(
        dense_kernel(mirrored),
        (ids, lists, counts),
        (1,),
        [whole(h.shape) for h in hams],
        whole(dims),
        shape(dims),
        hams,
        scratch=[pltpu.VMEM((48, B, B), bf16), pltpu.VMEM((96, B, B), f32)],
        flops=1 << 22,
        moved=5 << 20,
        room=32,
    )


rows = pl.BlockSpec((R, T), lambda i, *_: (i, 0))


def first_products_kernel(second):
    def kernel(ham_t_ref, ham_ref, x_ref, dr_ref, dc_ref, *refs):
        yk0_ref, yk1_ref = refs[8:10]
        out_ref, wide = refs[-2:]
        for i in range(8):
            wide[:, i * B : (i + 1) * B] = yk0_ref[i]
            wide[:, (8 + i) * B : (9 + i) * B] = yk1_ref[i]
        near = jnp.concatenate(
            [ref[0] for ref in refs[:4]] + [ref[m] for m in range(2) for ref in refs[4:8]], axis=0
        )
        total = jnp.dot(wide[...], ham_t_ref[...], preferred_element_type=f32) + jnp.dot(
            ham_ref[...], near, preferred_element_type=f32
        )
        total = total + (dr_ref[...] + dc_ref[...] - center) * x_ref[...]
        if second:
            total = total - refs[10][...] * (0.5 / scale)
        out_ref[...] = total

    return kernel


def first_products(ham_t, ham, value, dr, dc, x0, x12, yk0, yk1, before=None):
    extra = () if before is None else (before,)
    return call(
        first_products_kernel(before is not None),
        (),
        (T // R,),
        [
            whole((2048, T)),
            pl.BlockSpec((R, 1536), lambda i, *_: (i, 0)),
            rows,
            pl.BlockSpec((R, 1), lambda i, *_: (i, 0)),
            whole((1, T)),
        ]
        + [whole(s.shape) for s in x0 + x12]
        + [pl.BlockSpec((8, R, B), lambda i, *_: (0, i, 0))] * 2
        + [rows] * len(extra),
        rows,
        free_shape((T, T), f32),
        (ham_t, ham, value, dr, dc, *x0, *x12, yk0, yk1, *extra),
        scratch=[pltpu.VMEM((R, 2048), bf16)],
        flops=2 * T * T * 3584,
        moved=20 << 20,
        room=36,
        pinned=True,
    )


def finish_kernel(second):
    def kernel(ids, hot, sel, part_ref, ham_ref, *refs):
        stacked = jnp.concatenate([ref[0] for ref in refs[:4]], axis=0)
        out_ref = refs[4]
        total = part_ref[...] + jnp.dot(ham_ref[...], stacked, preferred_element_type=f32)
        if second:
            out_ref[...] = total * (2.0 * scale)
            return
        row_ref, col_ref = refs[5:7]
        out_ref[...] = total * scale
        i, r, c = pl.program_id(0), ids[0], ids[1]
        for h in range(2):
            col_ref[h] = out_ref[:, pl.ds(start(hot[c, h]), B)].astype(bf16)
            block = hot[r, h]

            @pl.when(block // 2 == i)
            def _(h=h, block=block):
                row_ref[h] = out_ref[pl.ds(start(block % 2), B), :].astype(bf16)

        choose_cols(ids, sel, 0, col_ref, refs[11])

        @pl.when(i == T // R - 1)
        def _():
            choose_rows(ids, sel, 0, row_ref, refs[7:11])

    return kernel


def finish(ids, hot, sel, part, ham, slabs, second):
    out_specs, out_shape = rows, shape((T, T), f32)
    if not second:
        out_specs = [rows, whole((2, B, T)), pl.BlockSpec((2, R, B), lambda i, *_: (0, i, 0))]
        out_specs += [whole((1, B, T))] * 4 + [pl.BlockSpec((8, R, B), lambda i, *_: (0, i, 0))]
        out_shape = [out_shape] + send_shapes
    return call(
        finish_kernel(second),
        (ids, hot, sel),
        (T // R,),
        [rows, pl.BlockSpec((R, 512), lambda i, *_: (i, 3))] + [whole((1, B, T))] * 4,
        out_specs,
        out_shape,
        (part, ham, *slabs),
        flops=2 * T * T * 512,
        moved=6 << 20,
        room=32,
    )


def body(start_vector, ham_blocks, diagonal, lists, counts, hot, sel):
    row_index = lax.axis_index("zl") * 4 + lax.axis_index("x")
    col_index = (lax.axis_index("zh") * 4 + lax.axis_index("y")) * 2 + lax.axis_index("k")
    ids = jnp.stack([row_index, col_index]).astype(jnp.int32)
    dr = lax.dynamic_slice_in_dim(diagonal, row_index * T, T).reshape(T, 1)
    dc = lax.dynamic_slice_in_dim(diagonal, col_index * T, T).reshape(1, T)

    piece = lax.dynamic_slice_in_dim(ham_blocks, col_index * 3, 3).transpose(0, 2, 1)
    piece = permute(piece, mirror)
    pieces = [piece] + [permute(piece, z_xor(n)) for n in (1, 2, 3)]
    row, col, *sends = pack(ids, hot, sel, start_vector)
    ham = dense(ids, lists, counts, (ham_blocks,), False)
    near = over_x(sends[:4])
    quarter, row, col, sends, near, ham, dr, dc = barrier(
        jnp.concatenate(pieces), row, col, sends, near, ham, dr, dc
    )
    ham_t = None
    outs = []
    value = start_vector
    for step in range(2):
        first = step == 0
        z1 = permute(row, z_xor(1))
        z2 = permute(row, z_xor(2))
        zh = permute(col, zh_flip)
        yk0 = over_yk(sends[4])
        if first:
            hams = [quarter] + [permute(quarter, x_shift(n)) for n in (1, 2)]
            sends = next_slabs(ids, sel, [z1, z2], (1, 2), zh)
            row, sends, near, yk0, hams = barrier(row, sends, near, yk0, hams)
            hams.append(permute(quarter, x_shift(3)))
        else:
            last = sends[3]
            near = [sends[0]] + [permute(sends[n], x_shift(n)) for n in (1, 2)]
            sends = next_slabs(ids, sel, [z1, z2], (1, 2), zh)
            row, sends, near, yk0, last = barrier(row, sends, near, yk0, last)
            near.append(permute(last, x_shift(3)))
        z3 = permute(row, z_xor(3))
        x12 = over_x(sends[:4])
        yk1 = over_yk(sends[4])
        if first:
            ham_t = dense(ids, lists, counts, hams, True)
        sends = next_slabs(ids, sel, [z3], (3,))
        sends, x12, yk1, near, ham_t = barrier(sends, x12, yk1, near, ham_t)
        x3 = over_x(sends)
        before = () if first else (start_vector,)
        part = first_products(ham_t, ham, value, dr, dc, near, x12, yk0, yk1, *before)
        result = finish(ids, hot, sel, part, ham, x3, not first)
        if first:
            value, *sent = result
            row, col, sends = barrier(sent[0], sent[1], sent[2:])
            result = value
        outs.append(result)
    return tuple(outs)


def solution(mesh):
    fine = Mesh(mesh.devices.reshape(sizes), axes)
    rows, cols = ("zl", "x"), ("zh", "y", "k")
    in_specs = (P(rows, cols), P(rows, None, None), P(), P(), P(), P(), P())
    out_specs = (P(rows, cols), P(rows, cols))
    return jax.shard_map(body, mesh=fine, in_specs=in_specs, out_specs=out_specs, check_vma=False)
```

```python
import jax
import jax.numpy as jnp
from jax import lax
from jax.experimental import pallas as pl
from jax.experimental.pallas import tpu as pltpu
from jax.sharding import Mesh, PartitionSpec as P
import numpy as np

center = 0.25
scale = 1.0 / 2.5
axes = ("zl", "x", "zh", "y", "k")
sizes = (4, 4, 2, 4, 2)
B = 128
T = 768
R = 256
bf16 = jnp.bfloat16
f32 = jnp.float32


def permute(value, target):
    places = list(np.ndindex(*sizes))
    pairs = [
        (int(np.ravel_multi_index(p, sizes)), int(np.ravel_multi_index(target(*p), sizes)))
        for p in places
    ]
    return lax.ppermute(value, axes, pairs)


def z_xor(n):
    return lambda zl, x, zh, y, k: (zl ^ n, x, zh, y, k)


def x_shift(n):
    return lambda zl, x, zh, y, k: (zl, (x + n) % 4, zh, y, k)


def zh_flip(zl, x, zh, y, k):
    return (zl, x, 1 - zh, y, k)


def mirror(zl, x, zh, y, k):
    r, c = zl * 4 + x, zh * 8 + y * 2 + k
    return (c // 4, c % 4, r // 8, (r % 8) // 2, r % 2)


def barrier(*values):
    return lax.optimization_barrier(values)


def after(value, earlier):
    return barrier(value, earlier)[0]


def start(block):
    return pl.multiple_of(block * B, B)


def call(kernel, scalars, grid, in_specs, out_specs, out_shape, args, scratch=(), flops=0, moved=0, room=1, pinned=False):
    return pl.pallas_call(
        kernel,
        grid_spec=pltpu.PrefetchScalarGridSpec(
            num_scalar_prefetch=len(scalars),
            grid=grid,
            in_specs=in_specs,
            out_specs=out_specs,
            scratch_shapes=list(scratch),
        ),
        out_shape=out_shape,
        compiler_params=pltpu.CompilerParams(vmem_limit_bytes=room << 20),
        cost_estimate=pl.CostEstimate(flops=flops, bytes_accessed=moved, transcendentals=0),
    )(*scalars, *(pltpu.with_memory_space_constraint(arg, pltpu.HBM) if pinned else arg for arg in args))


def shape(dims, kind=bf16):
    return pltpu.HBM(dims, kind)


def free_shape(dims, kind=bf16):
    return jax.ShapeDtypeStruct(dims, kind)


def whole(dims):
    return pl.BlockSpec(dims, lambda i, *_: (0,) * len(dims))


send_shapes = (
    [shape((2, B, T)), shape((2, T, B))] + [shape((1, B, T))] * 4 + [shape((8, T, B))]
)


def choose_rows(ids, sel, step, slabs_ref, refs, at=0):
    zl, x = ids[0] // 4, ids[0] % 4
    for n in range(4):
        refs[n][at] = slabs_ref[sel[zl * 4 + (x + n) % 4, (zl ^ step) * 4 + x]]


def choose_cols(ids, sel, flip, slabs_ref, out_ref):
    zh, q = ids[1] // 8, ids[1] ^ (8 * flip)
    for i in range(8):
        out_ref[i] = slabs_ref[sel[zh * 8 + i, q]]


def pack_kernel(ids, hot, sel, x_ref, row_ref, col_ref, *refs):
    r, c = ids[0], ids[1]
    for h in range(2):
        row_ref[h] = x_ref[pl.ds(start(hot[r, h]), B), :].astype(bf16)
        col_ref[h] = x_ref[:, pl.ds(start(hot[c, h]), B)].astype(bf16)
    choose_rows(ids, sel, 0, row_ref, refs[:4])
    choose_cols(ids, sel, 0, col_ref, refs[4])


def pack(ids, hot, sel, value):
    return call(
        pack_kernel,
        (ids, hot, sel),
        (1,),
        [whole((T, T))],
        [whole(s.shape) for s in send_shapes],
        send_shapes,
        (value,),
        moved=5 << 20,
        room=32,
    )


def next_slabs(ids, sel, rows, steps, cols=None):
    count = len(rows)

    def kernel(ids, sel, *refs):
        outs = refs[count + (cols is not None) :]
        for m in range(count):
            choose_rows(ids, sel, steps[m], refs[m], outs[:4], m)
        if cols is not None:
            choose_cols(ids, sel, 1, refs[count], outs[4])

    out_shapes = [shape((count, B, T))] * 4 + [shape((8, T, B))] * (cols is not None)
    args = rows if cols is None else rows + [cols]
    return call(
        kernel,
        (ids, sel),
        (1,),
        [whole(arg.shape) for arg in args],
        [whole(s.shape) for s in out_shapes],
        out_shapes,
        args,
        moved=4 << 20,
        room=32,
    )


def over_x(chosen):
    return [chosen[0]] + [permute(chosen[n], x_shift(n)) for n in (1, 2, 3)]


def over_yk(chosen):
    return lax.all_to_all(chosen, ("y", "k"), 0, 0, tiled=True)


def dense_kernel(mirrored):
    def kernel(ids, lists, counts, *refs):
        out_ref, held, total = refs[-3:]
        ham_ref = refs[0]
        r, c = ids[0], ids[1]
        tile = c if mirrored else r
        if mirrored:
            ham_ref = held
            for n in range(4):
                ham_ref[n * 12 : (n + 1) * 12] = refs[n][...]

        def clear(i, carry):
            total[i] = jnp.zeros((B, B), f32)
            return carry

        lax.fori_loop(0, 96, clear, 0)

        def add(slot, carry):
            q = lists[0, tile, slot]
            t = lists[1, tile, slot]
            b = lists[2, tile, slot]
            if mirrored:
                place = q ^ (c // 8 * 8)
                piece = b // 3
                b = ((r + 4 - piece % 4) % 4 * 4 + ((piece // 4) ^ (r // 4))) * 3 + b % 3
            else:
                place = ((q // 4) ^ (r // 4)) * 4 + (r + 4 - q % 4) % 4
            at = t * 16 + place
            total[at] = total[at] + ham_ref[b].astype(f32)
            return carry

        lax.fori_loop(0, counts[tile], add, 0)
        for t in range(6):
            for place in range(16):
                block = total[t * 16 + place].astype(bf16)
                if mirrored:
                    out_ref[place * B : (place + 1) * B, t * B : (t + 1) * B] = block
                else:
                    out_ref[t * B : (t + 1) * B, place * B : (place + 1) * B] = block

    return kernel


def dense(ids, lists, counts, hams, mirrored):
    dims = (2048, T) if mirrored else (T, 2048)
    return call(
        dense_kernel(mirrored),
        (ids, lists, counts),
        (1,),
        [whole(h.shape) for h in hams],
        whole(dims),
        shape(dims),
        hams,
        scratch=[pltpu.VMEM((48, B, B), bf16), pltpu.VMEM((96, B, B), f32)],
        flops=1 << 22,
        moved=5 << 20,
        room=32,
    )


rows = pl.BlockSpec((R, T), lambda i, *_: (i, 0))


def first_products_kernel(second):
    def kernel(ham_t_ref, ham_ref, x_ref, dr_ref, dc_ref, *refs):
        yk0_ref, yk1_ref = refs[8:10]
        out_ref, wide = refs[-2:]
        for i in range(8):
            wide[:, i * B : (i + 1) * B] = yk0_ref[i]
            wide[:, (8 + i) * B : (9 + i) * B] = yk1_ref[i]
        near = jnp.concatenate(
            [ref[0] for ref in refs[:4]] + [ref[m] for m in range(2) for ref in refs[4:8]], axis=0
        )
        total = jnp.dot(wide[...], ham_t_ref[...], preferred_element_type=f32) + jnp.dot(
            ham_ref[...], near, preferred_element_type=f32
        )
        total = total + (dr_ref[...] + dc_ref[...] - center) * x_ref[...]
        if second:
            total = total - refs[10][...] * (0.5 / scale)
        out_ref[...] = total

    return kernel


def first_products(ham_t, ham, value, dr, dc, x0, x12, yk0, yk1, before=None):
    extra = () if before is None else (before,)
    return call(
        first_products_kernel(before is not None),
        (),
        (T // R,),
        [
            whole((2048, T)),
            pl.BlockSpec((R, 1536), lambda i, *_: (i, 0)),
            rows,
            pl.BlockSpec((R, 1), lambda i, *_: (i, 0)),
            whole((1, T)),
        ]
        + [whole(s.shape) for s in x0 + x12]
        + [pl.BlockSpec((8, R, B), lambda i, *_: (0, i, 0))] * 2
        + [rows] * len(extra),
        rows,
        free_shape((T, T), f32),
        (ham_t, ham, value, dr, dc, *x0, *x12, yk0, yk1, *extra),
        scratch=[pltpu.VMEM((R, 2048), bf16)],
        flops=2 * T * T * 3584,
        moved=20 << 20,
        room=36,
        pinned=True,
    )


def finish_kernel(second):
    def kernel(ids, hot, sel, part_ref, ham_ref, *refs):
        stacked = jnp.concatenate([ref[0] for ref in refs[:4]], axis=0)
        out_ref = refs[4]
        total = part_ref[...] + jnp.dot(ham_ref[...], stacked, preferred_element_type=f32)
        if second:
            out_ref[...] = total * (2.0 * scale)
            return
        row_ref, col_ref = refs[5:7]
        out_ref[...] = total * scale
        i, r, c = pl.program_id(0), ids[0], ids[1]
        for h in range(2):
            col_ref[h] = out_ref[:, pl.ds(start(hot[c, h]), B)].astype(bf16)
            block = hot[r, h]

            @pl.when(block // 2 == i)
            def _(h=h, block=block):
                row_ref[h] = out_ref[pl.ds(start(block % 2), B), :].astype(bf16)

        choose_cols(ids, sel, 0, col_ref, refs[11])

        @pl.when(i == T // R - 1)
        def _():
            choose_rows(ids, sel, 0, row_ref, refs[7:11])

    return kernel


def finish(ids, hot, sel, part, ham, slabs, second):
    out_specs, out_shape = rows, shape((T, T), f32)
    if not second:
        out_specs = [rows, whole((2, B, T)), pl.BlockSpec((2, R, B), lambda i, *_: (0, i, 0))]
        out_specs += [whole((1, B, T))] * 4 + [pl.BlockSpec((8, R, B), lambda i, *_: (0, i, 0))]
        out_shape = [out_shape] + send_shapes
    return call(
        finish_kernel(second),
        (ids, hot, sel),
        (T // R,),
        [rows, pl.BlockSpec((R, 512), lambda i, *_: (i, 3))] + [whole((1, B, T))] * 4,
        out_specs,
        out_shape,
        (part, ham, *slabs),
        flops=2 * T * T * 512,
        moved=6 << 20,
        room=32,
    )


def body(start_vector, ham_blocks, diagonal, lists, counts, hot, sel):
    row_index = lax.axis_index("zl") * 4 + lax.axis_index("x")
    col_index = (lax.axis_index("zh") * 4 + lax.axis_index("y")) * 2 + lax.axis_index("k")
    ids = jnp.stack([row_index, col_index]).astype(jnp.int32)
    dr = lax.dynamic_slice_in_dim(diagonal, row_index * T, T).reshape(T, 1)
    dc = lax.dynamic_slice_in_dim(diagonal, col_index * T, T).reshape(1, T)

    piece = lax.dynamic_slice_in_dim(ham_blocks, col_index * 3, 3).transpose(0, 2, 1)
    piece = permute(piece, mirror)
    row, col, *sends = pack(ids, hot, sel, start_vector)
    zh = permute(col, zh_flip)
    piece, row, sends = barrier(piece, row, sends)
    near = [sends[0]] + [permute(sends[n], x_shift(n)) for n in (1, 2)]
    near.append(permute(after(sends[3], near[2]), x_shift(3)))
    pieces = [piece, permute(after(piece, near[1]), z_xor(1))]
    pieces += [permute(piece, z_xor(n)) for n in (2, 3)]
    ham = dense(ids, lists, counts, (ham_blocks,), False)
    quarter, row, zh, sends, near, ham, dr, dc = barrier(
        jnp.concatenate(pieces), row, zh, sends, near, ham, dr, dc
    )
    ham_t = None
    outs = []
    value = start_vector
    for step in range(2):
        first = step == 0
        z1 = permute(row, z_xor(1))
        z2 = permute(row, z_xor(2))
        yk0 = over_yk(sends[4])
        if first:
            hams = [quarter] + [permute(quarter, x_shift(n)) for n in (1, 2, 3)]
        else:
            zh = permute(col, zh_flip)
            near = [sends[0]] + [permute(sends[n], x_shift(n)) for n in (1, 2)]
            near.append(permute(after(sends[3], near[1]), x_shift(3)))
            hams = []
        sends = next_slabs(ids, sel, [z1, z2], (1, 2), zh)
        row, sends, near, yk0, hams = barrier(row, sends, near, yk0, hams)
        z3 = permute(row, z_xor(3))
        x12 = over_x(sends[:4])
        yk1 = over_yk(sends[4])
        if first:
            ham_t = dense(ids, lists, counts, hams, True)
        sends = next_slabs(ids, sel, [z3], (3,))
        sends, x12, yk1, near, ham_t = barrier(sends, x12, yk1, near, ham_t)
        x3 = over_x(sends)
        before = () if first else (start_vector,)
        part = first_products(ham_t, ham, value, dr, dc, near, x12, yk0, yk1, *before)
        result = finish(ids, hot, sel, part, ham, x3, not first)
        if first:
            value, *sent = result
            row, col, sends = barrier(sent[0], sent[1], sent[2:])
            result = value
        outs.append(result)
    return tuple(outs)


def solution(mesh):
    fine = Mesh(mesh.devices.reshape(sizes), axes)
    rows, cols = ("zl", "x"), ("zh", "y", "k")
    in_specs = (P(rows, cols), P(rows, None, None), P(), P(), P(), P(), P())
    out_specs = (P(rows, cols), P(rows, cols))
    return jax.shard_map(body, mesh=fine, in_specs=in_specs, out_specs=out_specs, check_vma=False)
```

```python
import jax
import jax.numpy as jnp
from jax import lax
from jax.experimental import pallas as pl
from jax.experimental.pallas import tpu as pltpu
from jax.sharding import Mesh, PartitionSpec as P
import numpy as np

center = 0.25
scale = 1.0 / 2.5
axes = ("zl", "x", "zh", "y", "k")
sizes = (4, 4, 2, 4, 2)
B = 128
T = 768
R = 256
bf16 = jnp.bfloat16
f32 = jnp.float32


def permute(value, target):
    places = list(np.ndindex(*sizes))
    pairs = [
        (int(np.ravel_multi_index(p, sizes)), int(np.ravel_multi_index(target(*p), sizes)))
        for p in places
    ]
    return lax.ppermute(value, axes, pairs)


def z_xor(n):
    return lambda zl, x, zh, y, k: (zl ^ n, x, zh, y, k)


def x_shift(n):
    return lambda zl, x, zh, y, k: (zl, (x + n) % 4, zh, y, k)


def zh_flip(zl, x, zh, y, k):
    return (zl, x, 1 - zh, y, k)


def mirror(zl, x, zh, y, k):
    r, c = zl * 4 + x, zh * 8 + y * 2 + k
    return (c // 4, c % 4, r // 8, (r % 8) // 2, r % 2)


def barrier(*values):
    return lax.optimization_barrier(values)


def after(value, earlier):
    return barrier(value, earlier)[0]


def start(block):
    return pl.multiple_of(block * B, B)


def call(kernel, scalars, grid, in_specs, out_specs, out_shape, args, scratch=(), flops=0, moved=0, room=1, pinned=False):
    return pl.pallas_call(
        kernel,
        grid_spec=pltpu.PrefetchScalarGridSpec(
            num_scalar_prefetch=len(scalars),
            grid=grid,
            in_specs=in_specs,
            out_specs=out_specs,
            scratch_shapes=list(scratch),
        ),
        out_shape=out_shape,
        compiler_params=pltpu.CompilerParams(vmem_limit_bytes=room << 20),
        cost_estimate=pl.CostEstimate(flops=flops, bytes_accessed=moved, transcendentals=0),
    )(*scalars, *(pltpu.with_memory_space_constraint(arg, pltpu.HBM) if pinned else arg for arg in args))


def shape(dims, kind=bf16):
    return pltpu.HBM(dims, kind)


def free_shape(dims, kind=bf16):
    return jax.ShapeDtypeStruct(dims, kind)


def whole(dims):
    return pl.BlockSpec(dims, lambda i, *_: (0,) * len(dims))


send_shapes = [shape((2, B, T)), shape((2, T, B))] + [shape((1, B, T))] * 4


def choose_rows(ids, sel, step, slabs_ref, refs, at=0):
    zl, x = ids[0] // 4, ids[0] % 4
    for n in range(4):
        refs[n][at] = slabs_ref[sel[zl * 4 + (x + n) % 4, (zl ^ step) * 4 + x]]


def pack_kernel(ids, hot, sel, x_ref, row_ref, col_ref, *refs):
    r, c = ids[0], ids[1]
    for h in range(2):
        row_ref[h] = x_ref[pl.ds(start(hot[r, h]), B), :].astype(bf16)
        col_ref[h] = x_ref[:, pl.ds(start(hot[c, h]), B)].astype(bf16)
    choose_rows(ids, sel, 0, row_ref, refs)


def pack(ids, hot, sel, value):
    return call(
        pack_kernel,
        (ids, hot, sel),
        (1,),
        [whole((T, T))],
        [whole(s.shape) for s in send_shapes],
        send_shapes,
        (value,),
        moved=5 << 20,
        room=32,
    )


def next_rows(ids, sel, rows, steps):
    count = len(rows)

    def kernel(ids, sel, *refs):
        for m in range(count):
            choose_rows(ids, sel, steps[m], refs[m], refs[count:], m)

    return call(
        kernel,
        (ids, sel),
        (1,),
        [whole(arg.shape) for arg in rows],
        [whole((count, B, T))] * 4,
        [shape((count, B, T))] * 4,
        rows,
        moved=4 << 20,
        room=32,
    )


def choose_cols(ids, sel, here, there):
    def kernel(ids, sel, here_ref, there_ref, out_ref):
        zh, q = ids[1] // 8, ids[1]
        for i in range(8):
            out_ref[2 * i] = here_ref[sel[zh * 8 + i, q]]
            out_ref[2 * i + 1] = there_ref[sel[zh * 8 + i, q ^ 8]]

    return call(
        kernel,
        (ids, sel),
        (1,),
        [whole(here.shape)] * 2,
        whole((16, T, B)),
        shape((16, T, B)),
        (here, there),
        moved=4 << 20,
        room=32,
    )


def over_x(chosen):
    return [chosen[0]] + [permute(chosen[n], x_shift(n)) for n in (1, 2, 3)]


def over_yk(chosen):
    return lax.all_to_all(chosen, ("y", "k"), 0, 0, tiled=True)


def dense_kernel(mirrored):
    def kernel(ids, lists, counts, *refs):
        out_ref, held, total = refs[-3:]
        ham_ref = refs[0]
        r, c = ids[0], ids[1]
        tile = c if mirrored else r
        if mirrored:
            ham_ref = held
            for n in range(4):
                ham_ref[n * 12 : (n + 1) * 12] = refs[n][...]

        def clear(i, carry):
            total[i] = jnp.zeros((B, B), f32)
            return carry

        lax.fori_loop(0, 96, clear, 0)

        def add(slot, carry):
            q = lists[0, tile, slot]
            t = lists[1, tile, slot]
            b = lists[2, tile, slot]
            if mirrored:
                place = q ^ (c // 8 * 8)
                piece = b // 3
                b = ((r + 4 - piece % 4) % 4 * 4 + ((piece // 4) ^ (r // 4))) * 3 + b % 3
            else:
                place = ((q // 4) ^ (r // 4)) * 4 + (r + 4 - q % 4) % 4
            at = t * 16 + place
            total[at] = total[at] + ham_ref[b].astype(f32)
            return carry

        lax.fori_loop(0, counts[tile], add, 0)
        for t in range(6):
            for place in range(16):
                block = total[t * 16 + place].astype(bf16)
                if mirrored:
                    out_ref[place * B : (place + 1) * B, t * B : (t + 1) * B] = block
                else:
                    out_ref[t * B : (t + 1) * B, place * B : (place + 1) * B] = block

    return kernel


def dense(ids, lists, counts, hams, mirrored):
    dims = (2048, T) if mirrored else (T, 2048)
    return call(
        dense_kernel(mirrored),
        (ids, lists, counts),
        (1,),
        [whole(h.shape) for h in hams],
        whole(dims),
        shape(dims),
        hams,
        scratch=[pltpu.VMEM((48, B, B), bf16), pltpu.VMEM((96, B, B), f32)],
        flops=1 << 22,
        moved=5 << 20,
        room=32,
    )


rows = pl.BlockSpec((R, T), lambda i, *_: (i, 0))


def first_products_kernel(second):
    def kernel(ham_t_ref, ham_ref, x_ref, dr_ref, dc_ref, *refs):
        yk_ref = refs[8]
        out_ref, wide = refs[-2:]
        for i in range(16):
            at = i % 2 * 8 + i // 2
            wide[:, at * B : (at + 1) * B] = yk_ref[i]
        near = jnp.concatenate(
            [ref[0] for ref in refs[:4]] + [ref[m] for m in range(2) for ref in refs[4:8]], axis=0
        )
        total = jnp.dot(wide[...], ham_t_ref[...], preferred_element_type=f32) + jnp.dot(
            ham_ref[...], near, preferred_element_type=f32
        )
        total = total + (dr_ref[...] + dc_ref[...] - center) * x_ref[...]
        if second:
            total = total - refs[9][...] * (0.5 / scale)
        out_ref[...] = total

    return kernel


def first_products(ham_t, ham, value, dr, dc, x0, x12, yk, before=None):
    extra = () if before is None else (before,)
    return call(
        first_products_kernel(before is not None),
        (),
        (T // R,),
        [
            whole((2048, T)),
            pl.BlockSpec((R, 1536), lambda i, *_: (i, 0)),
            rows,
            pl.BlockSpec((R, 1), lambda i, *_: (i, 0)),
            whole((1, T)),
        ]
        + [whole(s.shape) for s in x0 + x12]
        + [pl.BlockSpec((16, R, B), lambda i, *_: (0, i, 0))]
        + [rows] * len(extra),
        rows,
        free_shape((T, T), f32),
        (ham_t, ham, value, dr, dc, *x0, *x12, yk, *extra),
        scratch=[pltpu.VMEM((R, 2048), bf16)],
        flops=2 * T * T * 3584,
        moved=20 << 20,
        room=36,
        pinned=True,
    )


def finish_kernel(second):
    def kernel(ids, hot, sel, part_ref, ham_ref, *refs):
        stacked = jnp.concatenate([ref[0] for ref in refs[:4]], axis=0)
        out_ref = refs[4]
        total = part_ref[...] + jnp.dot(ham_ref[...], stacked, preferred_element_type=f32)
        if second:
            out_ref[...] = total * (2.0 * scale)
            return
        row_ref, col_ref = refs[5:7]
        out_ref[...] = total * scale
        i, r, c = pl.program_id(0), ids[0], ids[1]
        for h in range(2):
            col_ref[h] = out_ref[:, pl.ds(start(hot[c, h]), B)].astype(bf16)
            block = hot[r, h]

            @pl.when(block // 2 == i)
            def _(h=h, block=block):
                row_ref[h] = out_ref[pl.ds(start(block % 2), B), :].astype(bf16)

        @pl.when(i == T // R - 1)
        def _():
            choose_rows(ids, sel, 0, row_ref, refs[7:11])

    return kernel


def finish(ids, hot, sel, part, ham, slabs, second):
    out_specs, out_shape = rows, shape((T, T), f32)
    if not second:
        out_specs = [rows, whole((2, B, T)), pl.BlockSpec((2, R, B), lambda i, *_: (0, i, 0))]
        out_specs += [whole((1, B, T))] * 4
        out_shape = [out_shape] + send_shapes
    return call(
        finish_kernel(second),
        (ids, hot, sel),
        (T // R,),
        [rows, pl.BlockSpec((R, 512), lambda i, *_: (i, 3))] + [whole((1, B, T))] * 4,
        out_specs,
        out_shape,
        (part, ham, *slabs),
        flops=2 * T * T * 512,
        moved=6 << 20,
        room=32,
    )


def body(start_vector, ham_blocks, diagonal, lists, counts, hot, sel):
    row_index = lax.axis_index("zl") * 4 + lax.axis_index("x")
    col_index = (lax.axis_index("zh") * 4 + lax.axis_index("y")) * 2 + lax.axis_index("k")
    ids = jnp.stack([row_index, col_index]).astype(jnp.int32)
    dr = lax.dynamic_slice_in_dim(diagonal, row_index * T, T).reshape(T, 1)
    dc = lax.dynamic_slice_in_dim(diagonal, col_index * T, T).reshape(1, T)

    piece = lax.dynamic_slice_in_dim(ham_blocks, col_index * 3, 3).transpose(0, 2, 1)
    piece = permute(piece, mirror)
    row, col, *sends = pack(ids, hot, sel, start_vector)
    zh = permute(col, zh_flip)
    piece, row, sends = barrier(piece, row, sends)
    near = [sends[0]] + [permute(sends[n], x_shift(n)) for n in (1, 2)]
    near.append(permute(after(sends[3], near[2]), x_shift(3)))
    pieces = [piece, permute(after(piece, near[1]), z_xor(1))]
    pieces += [permute(piece, z_xor(n)) for n in (2, 3)]
    ham = dense(ids, lists, counts, (ham_blocks,), False)
    quarter, row, col, zh, near, ham, dr, dc = barrier(
        jnp.concatenate(pieces), row, col, zh, near, ham, dr, dc
    )
    ham_t = None
    outs = []
    value = start_vector
    for step in range(2):
        first = step == 0
        if not first:
            zh = permute(col, zh_flip)
            near = over_x(sends)
            row, col, zh, near = barrier(row, col, zh, near)
        z1 = permute(row, z_xor(1))
        z2 = permute(row, z_xor(2))
        yk = over_yk(choose_cols(ids, sel, col, zh))
        hams = over_x([quarter] * 4) if first else []
        far = next_rows(ids, sel, [z1, z2], (1, 2))
        row, far, hams = barrier(row, far, hams)
        z3 = permute(row, z_xor(3))
        x12 = over_x(far)
        if first:
            ham_t = dense(ids, lists, counts, hams, True)
        far = next_rows(ids, sel, [z3], (3,))
        far, x12, ham_t = barrier(far, x12, ham_t)
        x3 = over_x(far)
        before = () if first else (start_vector,)
        part = first_products(ham_t, ham, value, dr, dc, near, x12, yk, *before)
        result = finish(ids, hot, sel, part, ham, x3, not first)
        if first:
            value, *sent = result
            row, col, sends = barrier(sent[0], sent[1], sent[2:])
            result = value
        outs.append(result)
    return tuple(outs)


def solution(mesh):
    fine = Mesh(mesh.devices.reshape(sizes), axes)
    rows, cols = ("zl", "x"), ("zh", "y", "k")
    in_specs = (P(rows, cols), P(rows, None, None), P(), P(), P(), P(), P())
    out_specs = (P(rows, cols), P(rows, cols))
    return jax.shard_map(body, mesh=fine, in_specs=in_specs, out_specs=out_specs, check_vma=False)
```

```python
import jax
import jax.numpy as jnp
from jax import lax
from jax.experimental import pallas as pl
from jax.experimental.pallas import tpu as pltpu
from jax.sharding import Mesh, PartitionSpec as P
import numpy as np

center = 0.25
scale = 1.0 / 2.5
axes = ("zl", "x", "zh", "y", "k")
sizes = (4, 4, 2, 4, 2)
B = 128
T = 768
R = 256
bf16 = jnp.bfloat16
f32 = jnp.float32


def permute(value, target):
    places = list(np.ndindex(*sizes))
    pairs = [
        (int(np.ravel_multi_index(p, sizes)), int(np.ravel_multi_index(target(*p), sizes)))
        for p in places
    ]
    return lax.ppermute(value, axes, pairs)


def z_xor(n):
    return lambda zl, x, zh, y, k: (zl ^ n, x, zh, y, k)


def x_shift(n):
    return lambda zl, x, zh, y, k: (zl, (x + n) % 4, zh, y, k)


def zh_flip(zl, x, zh, y, k):
    return (zl, x, 1 - zh, y, k)


def mirror(zl, x, zh, y, k):
    r, c = zl * 4 + x, zh * 8 + y * 2 + k
    return (c // 4, c % 4, r // 8, (r % 8) // 2, r % 2)


def barrier(*values):
    return lax.optimization_barrier(values)


def after(value, earlier):
    return barrier(value, earlier)[0]


def start(block):
    return pl.multiple_of(block * B, B)


def call(kernel, scalars, grid, in_specs, out_specs, out_shape, args, scratch=(), flops=0, moved=0, room=1, pinned=False):
    return pl.pallas_call(
        kernel,
        grid_spec=pltpu.PrefetchScalarGridSpec(
            num_scalar_prefetch=len(scalars),
            grid=grid,
            in_specs=in_specs,
            out_specs=out_specs,
            scratch_shapes=list(scratch),
        ),
        out_shape=out_shape,
        compiler_params=pltpu.CompilerParams(vmem_limit_bytes=room << 20),
        cost_estimate=pl.CostEstimate(flops=flops, bytes_accessed=moved, transcendentals=0),
    )(*scalars, *(pltpu.with_memory_space_constraint(arg, pltpu.HBM) if pinned else arg for arg in args))


def shape(dims, kind=bf16):
    return pltpu.HBM(dims, kind)


def free_shape(dims, kind=bf16):
    return jax.ShapeDtypeStruct(dims, kind)


def whole(dims):
    return pl.BlockSpec(dims, lambda i, *_: (0,) * len(dims))


send_shapes = [shape((2, B, T)), shape((2, T, B))] + [shape((1, B, T))] * 4


def choose_rows(ids, sel, step, slabs_ref, refs, at=0):
    zl, x = ids[0] // 4, ids[0] % 4
    for n in range(4):
        refs[n][at] = slabs_ref[sel[zl * 4 + (x + n) % 4, (zl ^ step) * 4 + x]]


def pack_kernel(ids, hot, sel, x_ref, row_ref, col_ref, *refs):
    r, c = ids[0], ids[1]
    for h in range(2):
        row_ref[h] = x_ref[pl.ds(start(hot[r, h]), B), :].astype(bf16)
        col_ref[h] = x_ref[:, pl.ds(start(hot[c, h]), B)].astype(bf16)
    choose_rows(ids, sel, 0, row_ref, refs)


def pack(ids, hot, sel, value):
    return call(
        pack_kernel,
        (ids, hot, sel),
        (1,),
        [whole((T, T))],
        [whole(s.shape) for s in send_shapes],
        send_shapes,
        (value,),
        moved=5 << 20,
        room=32,
    )


def next_rows(ids, sel, rows, steps):
    count = len(rows)

    def kernel(ids, sel, *refs):
        for m in range(count):
            choose_rows(ids, sel, steps[m], refs[m], refs[count:], m)

    return call(
        kernel,
        (ids, sel),
        (1,),
        [whole(arg.shape) for arg in rows],
        [whole((count, B, T))] * 4,
        [shape((count, B, T))] * 4,
        rows,
        moved=4 << 20,
        room=32,
    )


def choose_cols(ids, sel, here, there):
    def kernel(ids, sel, here_ref, there_ref, out_ref):
        zh, q = ids[1] // 8, ids[1]
        for i in range(8):
            out_ref[2 * i] = here_ref[sel[zh * 8 + i, q]]
            out_ref[2 * i + 1] = there_ref[sel[zh * 8 + i, q ^ 8]]

    return call(
        kernel,
        (ids, sel),
        (1,),
        [whole(here.shape)] * 2,
        whole((16, T, B)),
        shape((16, T, B)),
        (here, there),
        moved=4 << 20,
        room=32,
    )


def over_x(chosen):
    return [chosen[0]] + [permute(chosen[n], x_shift(n)) for n in (1, 2, 3)]


def over_yk(chosen):
    return lax.all_to_all(chosen, ("y", "k"), 0, 0, tiled=True)


def dense_kernel(mirrored):
    def kernel(ids, lists, counts, *refs):
        out_ref, held, total = refs[-3:]
        ham_ref = refs[0]
        r, c = ids[0], ids[1]
        tile = c if mirrored else r
        if mirrored:
            ham_ref = held
            for n in range(4):
                ham_ref[n * 12 : (n + 1) * 12] = refs[n][...]

        def clear(i, carry):
            total[i] = jnp.zeros((B, B), f32)
            return carry

        lax.fori_loop(0, 96, clear, 0)

        def add(slot, carry):
            q = lists[0, tile, slot]
            t = lists[1, tile, slot]
            b = lists[2, tile, slot]
            if mirrored:
                place = q ^ (c // 8 * 8)
                piece = b // 3
                b = ((r + 4 - piece % 4) % 4 * 4 + ((piece // 4) ^ (r // 4))) * 3 + b % 3
            else:
                place = ((q // 4) ^ (r // 4)) * 4 + (r + 4 - q % 4) % 4
            at = t * 16 + place
            total[at] = total[at] + ham_ref[b].astype(f32)
            return carry

        lax.fori_loop(0, counts[tile], add, 0)
        for t in range(6):
            for place in range(16):
                block = total[t * 16 + place].astype(bf16)
                if mirrored:
                    out_ref[place * B : (place + 1) * B, t * B : (t + 1) * B] = block
                else:
                    out_ref[t * B : (t + 1) * B, place * B : (place + 1) * B] = block

    return kernel


def dense(ids, lists, counts, hams, mirrored):
    dims = (2048, T) if mirrored else (T, 2048)
    return call(
        dense_kernel(mirrored),
        (ids, lists, counts),
        (1,),
        [whole(h.shape) for h in hams],
        whole(dims),
        shape(dims),
        hams,
        scratch=[pltpu.VMEM((48, B, B), bf16), pltpu.VMEM((96, B, B), f32)],
        flops=1 << 22,
        moved=5 << 20,
        room=32,
    )


rows = pl.BlockSpec((R, T), lambda i, *_: (i, 0))


def first_products_kernel(second):
    def kernel(ham_t_ref, ham_ref, x_ref, dr_ref, dc_ref, *refs):
        yk_ref = refs[8]
        out_ref, wide = refs[-2:]
        for i in range(16):
            at = i % 2 * 8 + i // 2
            wide[:, at * B : (at + 1) * B] = yk_ref[i]
        near = jnp.concatenate(
            [ref[0] for ref in refs[:4]] + [ref[m] for m in range(2) for ref in refs[4:8]], axis=0
        )
        total = jnp.dot(wide[...], ham_t_ref[...], preferred_element_type=f32) + jnp.dot(
            ham_ref[...], near, preferred_element_type=f32
        )
        total = total + (dr_ref[...] + dc_ref[...] - center) * x_ref[...]
        if second:
            total = total - refs[9][...] * (0.5 / scale)
        out_ref[...] = total

    return kernel


def first_products(ham_t, ham, value, dr, dc, x0, x12, yk, before=None):
    extra = () if before is None else (before,)
    return call(
        first_products_kernel(before is not None),
        (),
        (T // R,),
        [
            whole((2048, T)),
            pl.BlockSpec((R, 1536), lambda i, *_: (i, 0)),
            rows,
            pl.BlockSpec((R, 1), lambda i, *_: (i, 0)),
            whole((1, T)),
        ]
        + [whole(s.shape) for s in x0 + x12]
        + [pl.BlockSpec((16, R, B), lambda i, *_: (0, i, 0))]
        + [rows] * len(extra),
        rows,
        free_shape((T, T), f32),
        (ham_t, ham, value, dr, dc, *x0, *x12, yk, *extra),
        scratch=[pltpu.VMEM((R, 2048), bf16)],
        flops=2 * T * T * 3584,
        moved=20 << 20,
        room=36,
        pinned=True,
    )


def finish_kernel(second):
    def kernel(ids, hot, sel, part_ref, ham_ref, *refs):
        stacked = jnp.concatenate([ref[0] for ref in refs[:4]], axis=0)
        out_ref = refs[4]
        total = part_ref[...] + jnp.dot(ham_ref[...], stacked, preferred_element_type=f32)
        if second:
            out_ref[...] = total * (2.0 * scale)
            return
        row_ref, col_ref = refs[5:7]
        out_ref[...] = total * scale
        i, r, c = pl.program_id(0), ids[0], ids[1]
        for h in range(2):
            col_ref[h] = out_ref[:, pl.ds(start(hot[c, h]), B)].astype(bf16)
            block = hot[r, h]

            @pl.when(block // 2 == i)
            def _(h=h, block=block):
                row_ref[h] = out_ref[pl.ds(start(block % 2), B), :].astype(bf16)

        @pl.when(i == T // R - 1)
        def _():
            choose_rows(ids, sel, 0, row_ref, refs[7:11])

    return kernel


def finish(ids, hot, sel, part, ham, slabs, second):
    out_specs, out_shape = rows, shape((T, T), f32)
    if not second:
        out_specs = [rows, whole((2, B, T)), pl.BlockSpec((2, R, B), lambda i, *_: (0, i, 0))]
        out_specs += [whole((1, B, T))] * 4
        out_shape = [out_shape] + send_shapes
    return call(
        finish_kernel(second),
        (ids, hot, sel),
        (T // R,),
        [rows, pl.BlockSpec((R, 512), lambda i, *_: (i, 3))] + [whole((1, B, T))] * 4,
        out_specs,
        out_shape,
        (part, ham, *slabs),
        flops=2 * T * T * 512,
        moved=6 << 20,
        room=32,
    )


def body(start_vector, ham_blocks, diagonal, lists, counts, hot, sel):
    row_index = lax.axis_index("zl") * 4 + lax.axis_index("x")
    col_index = (lax.axis_index("zh") * 4 + lax.axis_index("y")) * 2 + lax.axis_index("k")
    ids = jnp.stack([row_index, col_index]).astype(jnp.int32)
    dr = lax.dynamic_slice_in_dim(diagonal, row_index * T, T).reshape(T, 1)
    dc = lax.dynamic_slice_in_dim(diagonal, col_index * T, T).reshape(1, T)

    piece = lax.dynamic_slice_in_dim(ham_blocks, col_index * 3, 3).transpose(0, 2, 1)
    row, col, *sends = pack(ids, hot, sel, start_vector)
    zh = permute(col, zh_flip)
    piece = permute(after(piece, row), mirror)
    near = [sends[0]] + [permute(sends[n], x_shift(n)) for n in (1, 2)]
    near.append(permute(after(sends[3], near[1]), x_shift(3)))
    pieces = [piece, permute(after(piece, zh), z_xor(1))]
    pieces += [permute(piece, z_xor(n)) for n in (2, 3)]
    ham = dense(ids, lists, counts, (ham_blocks,), False)
    quarter, row, col, zh, near, ham, dr, dc = barrier(
        jnp.concatenate(pieces), row, col, zh, near, ham, dr, dc
    )
    ham_t = None
    outs = []
    value = start_vector
    for step in range(2):
        first = step == 0
        if not first:
            zh = permute(col, zh_flip)
            near = over_x(sends)
            row, col, zh, near = barrier(row, col, zh, near)
        z1 = permute(row, z_xor(1))
        z2 = permute(row, z_xor(2))
        yk = over_yk(choose_cols(ids, sel, col, zh))
        hams = over_x([quarter] * 4) if first else []
        far = next_rows(ids, sel, [z1, z2], (1, 2))
        row, far, hams = barrier(row, far, hams)
        z3 = permute(row, z_xor(3))
        x12 = over_x(far)
        if first:
            ham_t = dense(ids, lists, counts, hams, True)
        far = next_rows(ids, sel, [z3], (3,))
        far, x12, ham_t = barrier(far, x12, ham_t)
        x3 = over_x(far)
        before = () if first else (start_vector,)
        part = first_products(ham_t, ham, value, dr, dc, near, x12, yk, *before)
        result = finish(ids, hot, sel, part, ham, x3, not first)
        if first:
            value, *sent = result
            row, col, sends = barrier(sent[0], sent[1], sent[2:])
            result = value
        outs.append(result)
    return tuple(outs)


def solution(mesh):
    fine = Mesh(mesh.devices.reshape(sizes), axes)
    rows, cols = ("zl", "x"), ("zh", "y", "k")
    in_specs = (P(rows, cols), P(rows, None, None), P(), P(), P(), P(), P())
    out_specs = (P(rows, cols), P(rows, cols))
    return jax.shard_map(body, mesh=fine, in_specs=in_specs, out_specs=out_specs, check_vma=False)
```

```python
import jax
import jax.numpy as jnp
from jax import lax
from jax.experimental import pallas as pl
from jax.experimental.pallas import tpu as pltpu
from jax.sharding import Mesh, PartitionSpec as P
import numpy as np

center = 0.25
scale = 1.0 / 2.5
axes = ("zl", "x", "zh", "y", "k")
sizes = (4, 4, 2, 4, 2)
B = 128
T = 768
R = 256
bf16 = jnp.bfloat16
f32 = jnp.float32


def permute(value, target):
    places = list(np.ndindex(*sizes))
    pairs = [
        (int(np.ravel_multi_index(p, sizes)), int(np.ravel_multi_index(target(*p), sizes)))
        for p in places
    ]
    return lax.ppermute(value, axes, pairs)


def z_xor(n):
    return lambda zl, x, zh, y, k: (zl ^ n, x, zh, y, k)


def x_shift(n):
    return lambda zl, x, zh, y, k: (zl, (x + n) % 4, zh, y, k)


def zh_flip(zl, x, zh, y, k):
    return (zl, x, 1 - zh, y, k)


def mirror(zl, x, zh, y, k):
    r, c = zl * 4 + x, zh * 8 + y * 2 + k
    return (c // 4, c % 4, r // 8, (r % 8) // 2, r % 2)


def barrier(*values):
    return lax.optimization_barrier(values)


def after(value, earlier):
    return barrier(value, earlier)[0]


def start(block):
    return pl.multiple_of(block * B, B)


def call(kernel, scalars, grid, in_specs, out_specs, out_shape, args, scratch=(), flops=0, moved=0, room=1, pinned=False):
    return pl.pallas_call(
        kernel,
        grid_spec=pltpu.PrefetchScalarGridSpec(
            num_scalar_prefetch=len(scalars),
            grid=grid,
            in_specs=in_specs,
            out_specs=out_specs,
            scratch_shapes=list(scratch),
        ),
        out_shape=out_shape,
        compiler_params=pltpu.CompilerParams(vmem_limit_bytes=room << 20),
        cost_estimate=pl.CostEstimate(flops=flops, bytes_accessed=moved, transcendentals=0),
    )(*scalars, *(pltpu.with_memory_space_constraint(arg, pltpu.HBM) if pinned else arg for arg in args))


def shape(dims, kind=bf16):
    return pltpu.HBM(dims, kind)


def free_shape(dims, kind=bf16):
    return jax.ShapeDtypeStruct(dims, kind)


def whole(dims):
    return pl.BlockSpec(dims, lambda i, *_: (0,) * len(dims))


send_shapes = [shape((2, B, T)), shape((2, T, B))] + [shape((1, B, T))] * 4


def choose_rows(ids, sel, step, slabs_ref, refs, at=0):
    zl, x = ids[0] // 4, ids[0] % 4
    for n in range(4):
        refs[n][at] = slabs_ref[sel[zl * 4 + (x + n) % 4, (zl ^ step) * 4 + x]]


def pack_kernel(ids, hot, sel, x_ref, row_ref, col_ref, *refs):
    r, c = ids[0], ids[1]
    for h in range(2):
        row_ref[h] = x_ref[pl.ds(start(hot[r, h]), B), :].astype(bf16)
        col_ref[h] = x_ref[:, pl.ds(start(hot[c, h]), B)].astype(bf16)
    choose_rows(ids, sel, 0, row_ref, refs)


def pack(ids, hot, sel, value):
    return call(
        pack_kernel,
        (ids, hot, sel),
        (1,),
        [whole((T, T))],
        [whole(s.shape) for s in send_shapes],
        send_shapes,
        (value,),
        moved=5 << 20,
        room=32,
    )


def next_rows(ids, sel, rows, steps):
    count = len(rows)

    def kernel(ids, sel, *refs):
        for m in range(count):
            choose_rows(ids, sel, steps[m], refs[m], refs[count:], m)

    return call(
        kernel,
        (ids, sel),
        (1,),
        [whole(arg.shape) for arg in rows],
        [whole((count, B, T))] * 4,
        [shape((count, B, T))] * 4,
        rows,
        moved=4 << 20,
        room=32,
    )


def choose_cols(ids, sel, here, there):
    def kernel(ids, sel, here_ref, there_ref, out_ref):
        zh, q = ids[1] // 8, ids[1]
        for i in range(8):
            out_ref[2 * i] = here_ref[sel[zh * 8 + i, q]]
            out_ref[2 * i + 1] = there_ref[sel[zh * 8 + i, q ^ 8]]

    return call(
        kernel,
        (ids, sel),
        (1,),
        [whole(here.shape)] * 2,
        whole((16, T, B)),
        shape((16, T, B)),
        (here, there),
        moved=4 << 20,
        room=32,
    )


def over_x(chosen):
    return [chosen[0]] + [permute(chosen[n], x_shift(n)) for n in (1, 2, 3)]


def over_yk(chosen):
    return lax.all_to_all(chosen, ("y", "k"), 0, 0, tiled=True)


def dense_kernel(mirrored):
    def kernel(ids, lists, counts, *refs):
        out_ref, held, total = refs[-3:]
        ham_ref = refs[0]
        r, c = ids[0], ids[1]
        tile = c if mirrored else r
        if mirrored:
            ham_ref = held
            for n in range(4):
                ham_ref[n * 12 : (n + 1) * 12] = refs[n][...]

        def clear(i, carry):
            total[i] = jnp.zeros((B, B), f32)
            return carry

        lax.fori_loop(0, 96, clear, 0)

        def add(slot, carry):
            q = lists[0, tile, slot]
            t = lists[1, tile, slot]
            b = lists[2, tile, slot]
            if mirrored:
                place = q ^ (c // 8 * 8)
                piece = b // 3
                b = ((r + 4 - piece % 4) % 4 * 4 + ((piece // 4) ^ (r // 4))) * 3 + b % 3
            else:
                place = ((q // 4) ^ (r // 4)) * 4 + (r + 4 - q % 4) % 4
            at = t * 16 + place
            total[at] = total[at] + ham_ref[b].astype(f32)
            return carry

        lax.fori_loop(0, counts[tile], add, 0)
        for t in range(6):
            for place in range(16):
                block = total[t * 16 + place].astype(bf16)
                if mirrored:
                    out_ref[place * B : (place + 1) * B, t * B : (t + 1) * B] = block
                else:
                    out_ref[t * B : (t + 1) * B, place * B : (place + 1) * B] = block

    return kernel


def dense(ids, lists, counts, hams, mirrored):
    dims = (2048, T) if mirrored else (T, 2048)
    return call(
        dense_kernel(mirrored),
        (ids, lists, counts),
        (1,),
        [whole(h.shape) for h in hams],
        whole(dims),
        shape(dims),
        hams,
        scratch=[pltpu.VMEM((48, B, B), bf16), pltpu.VMEM((96, B, B), f32)],
        flops=1 << 22,
        moved=5 << 20,
        room=32,
    )


rows = pl.BlockSpec((R, T), lambda i, *_: (i, 0))


def first_products_kernel(second):
    def kernel(ham_t_ref, ham_ref, x_ref, dr_ref, dc_ref, *refs):
        yk_ref = refs[8]
        out_ref, wide = refs[-2:]
        for i in range(16):
            at = i % 2 * 8 + i // 2
            wide[:, at * B : (at + 1) * B] = yk_ref[i]
        near = jnp.concatenate(
            [ref[0] for ref in refs[:4]] + [ref[m] for m in range(2) for ref in refs[4:8]], axis=0
        )
        total = jnp.dot(wide[...], ham_t_ref[...], preferred_element_type=f32) + jnp.dot(
            ham_ref[...], near, preferred_element_type=f32
        )
        total = total + (dr_ref[...] + dc_ref[...] - center) * x_ref[...]
        if second:
            total = total - refs[9][...] * (0.5 / scale)
        out_ref[...] = total

    return kernel


def first_products(ham_t, ham, value, dr, dc, x0, x12, yk, before=None):
    extra = () if before is None else (before,)
    return call(
        first_products_kernel(before is not None),
        (),
        (T // R,),
        [
            whole((2048, T)),
            pl.BlockSpec((R, 1536), lambda i, *_: (i, 0)),
            rows,
            pl.BlockSpec((R, 1), lambda i, *_: (i, 0)),
            whole((1, T)),
        ]
        + [whole(s.shape) for s in x0 + x12]
        + [pl.BlockSpec((16, R, B), lambda i, *_: (0, i, 0))]
        + [rows] * len(extra),
        rows,
        free_shape((T, T), f32),
        (ham_t, ham, value, dr, dc, *x0, *x12, yk, *extra),
        scratch=[pltpu.VMEM((R, 2048), bf16)],
        flops=2 * T * T * 3584,
        moved=20 << 20,
        room=36,
        pinned=True,
    )


def hot_kernel(ids, hot, sel, part_ref, ham_ref, *refs):
    slabs, row_ref, col_ref = refs[:4], refs[4], refs[5]
    r, c = ids[0], ids[1]
    stacked = jnp.concatenate([ref[0] for ref in slabs], axis=0)
    for h in range(2):
        at = pl.ds(start(hot[r, h]), B)
        total = part_ref[at, :] + jnp.dot(ham_ref[at, :], stacked, preferred_element_type=f32)
        row_ref[h] = (total * scale).astype(bf16)
        at = pl.ds(start(hot[c, h]), B)
        some = jnp.concatenate([ref[0, :, at] for ref in slabs], axis=0)
        total = part_ref[:, at] + jnp.dot(ham_ref[...], some, preferred_element_type=f32)
        col_ref[h] = (total * scale).astype(bf16)
    choose_rows(ids, sel, 0, row_ref, refs[6:])


def finish_hot(ids, hot, sel, part, ham, slabs):
    return call(
        hot_kernel,
        (ids, hot, sel),
        (1,),
        [whole((T, T)), pl.BlockSpec((T, 512), lambda i, *_: (0, 3))] + [whole((1, B, T))] * 4,
        [whole(s.shape) for s in send_shapes],
        send_shapes,
        (part, ham, *slabs),
        flops=2 * T * 512 * 512,
        moved=6 << 20,
        room=32,
    )


def finish_kernel(factor):
    def kernel(part_ref, ham_ref, *refs):
        stacked = jnp.concatenate([ref[0] for ref in refs[:4]], axis=0)
        total = part_ref[...] + jnp.dot(ham_ref[...], stacked, preferred_element_type=f32)
        refs[4][...] = total * factor

    return kernel


def finish(part, ham, slabs, factor):
    return call(
        finish_kernel(factor),
        (),
        (T // R,),
        [rows, pl.BlockSpec((R, 512), lambda i, *_: (i, 3))] + [whole((1, B, T))] * 4,
        rows,
        shape((T, T), f32),
        (part, ham, *slabs),
        flops=2 * T * T * 512,
        moved=6 << 20,
        room=32,
    )


def body(start_vector, ham_blocks, diagonal, lists, counts, hot, sel):
    row_index = lax.axis_index("zl") * 4 + lax.axis_index("x")
    col_index = (lax.axis_index("zh") * 4 + lax.axis_index("y")) * 2 + lax.axis_index("k")
    ids = jnp.stack([row_index, col_index]).astype(jnp.int32)
    dr = lax.dynamic_slice_in_dim(diagonal, row_index * T, T).reshape(T, 1)
    dc = lax.dynamic_slice_in_dim(diagonal, col_index * T, T).reshape(1, T)

    piece = lax.dynamic_slice_in_dim(ham_blocks, col_index * 3, 3).transpose(0, 2, 1)
    row, col, *sends = pack(ids, hot, sel, start_vector)
    zh = permute(col, zh_flip)
    piece = permute(after(piece, row), mirror)
    near = [sends[0]] + [permute(sends[n], x_shift(n)) for n in (1, 2)]
    near.append(permute(after(sends[3], [near[1], piece]), x_shift(3)))
    pieces = [piece, permute(after(piece, [zh, near]), z_xor(1))]
    pieces += [permute(piece, z_xor(n)) for n in (2, 3)]
    ham = dense(ids, lists, counts, (ham_blocks,), False)
    quarter, row, col, zh, near = barrier(jnp.concatenate(pieces), row, col, zh, near)
    ham_t = None
    outs = []
    value = start_vector
    for step in range(2):
        first = step == 0
        if not first:
            zh = permute(col, zh_flip)
            near = over_x(sends)
            row, col, zh, near, value = barrier(row, col, zh, near, value)
            outs.append(value)
        z1 = permute(row, z_xor(1))
        z2 = permute(row, z_xor(2))
        yk = over_yk(choose_cols(ids, sel, col, zh))
        hams = over_x([quarter] * 4) if first else []
        far = next_rows(ids, sel, [z1, z2], (1, 2))
        row, far, hams, ham, dr, dc = barrier(row, far, hams, ham, dr, dc)
        z3 = permute(row, z_xor(3))
        x12 = over_x(far)
        if first:
            ham_t = dense(ids, lists, counts, hams, True)
        far = next_rows(ids, sel, [z3], (3,))
        far, x12, ham_t = barrier(far, x12, ham_t)
        x3 = over_x(far)
        before = () if first else (start_vector,)
        part = first_products(ham_t, ham, value, dr, dc, near, x12, yk, *before)
        if first:
            row, col, *sends = finish_hot(ids, hot, sel, part, ham, x3)
            value = finish(part, ham, x3, scale)
        else:
            outs.append(finish(part, ham, x3, 2.0 * scale))
    return tuple(outs)


def solution(mesh):
    fine = Mesh(mesh.devices.reshape(sizes), axes)
    rows, cols = ("zl", "x"), ("zh", "y", "k")
    in_specs = (P(rows, cols), P(rows, None, None), P(), P(), P(), P(), P())
    out_specs = (P(rows, cols), P(rows, cols))
    return jax.shard_map(body, mesh=fine, in_specs=in_specs, out_specs=out_specs, check_vma=False)
```

```python
import jax
import jax.numpy as jnp
from jax import lax
from jax.experimental import pallas as pl
from jax.experimental.pallas import tpu as pltpu
from jax.sharding import Mesh, PartitionSpec as P
import numpy as np

center = 0.25
scale = 1.0 / 2.5
axes = ("zl", "x", "zh", "y", "k")
sizes = (4, 4, 2, 4, 2)
B = 128
T = 768
R = 256
bf16 = jnp.bfloat16
f32 = jnp.float32


def permute(value, target):
    places = list(np.ndindex(*sizes))
    pairs = [
        (int(np.ravel_multi_index(p, sizes)), int(np.ravel_multi_index(target(*p), sizes)))
        for p in places
    ]
    return lax.ppermute(value, axes, pairs)


def z_xor(n):
    return lambda zl, x, zh, y, k: (zl ^ n, x, zh, y, k)


def x_shift(n):
    return lambda zl, x, zh, y, k: (zl, (x + n) % 4, zh, y, k)


def zh_flip(zl, x, zh, y, k):
    return (zl, x, 1 - zh, y, k)


def mirror(zl, x, zh, y, k):
    r, c = zl * 4 + x, zh * 8 + y * 2 + k
    return (c // 4, c % 4, r // 8, (r % 8) // 2, r % 2)


def barrier(*values):
    return lax.optimization_barrier(values)


def after(value, earlier):
    return barrier(value, earlier)[0]


def start(block):
    return pl.multiple_of(block * B, B)


def call(kernel, scalars, grid, in_specs, out_specs, out_shape, args, scratch=(), flops=0, moved=0, room=1, pinned=False):
    return pl.pallas_call(
        kernel,
        grid_spec=pltpu.PrefetchScalarGridSpec(
            num_scalar_prefetch=len(scalars),
            grid=grid,
            in_specs=in_specs,
            out_specs=out_specs,
            scratch_shapes=list(scratch),
        ),
        out_shape=out_shape,
        compiler_params=pltpu.CompilerParams(vmem_limit_bytes=room << 20),
        cost_estimate=pl.CostEstimate(flops=flops, bytes_accessed=moved, transcendentals=0),
    )(*scalars, *(pltpu.with_memory_space_constraint(arg, pltpu.HBM) if pinned else arg for arg in args))


def shape(dims, kind=bf16):
    return pltpu.HBM(dims, kind)


def free_shape(dims, kind=bf16):
    return jax.ShapeDtypeStruct(dims, kind)


def whole(dims):
    return pl.BlockSpec(dims, lambda i, *_: (0,) * len(dims))


send_shapes = [shape((2, B, T)), shape((2, T, B))] + [shape((1, B, T))] * 4


def choose_rows(ids, sel, step, slabs_ref, refs, at=0):
    zl, x = ids[0] // 4, ids[0] % 4
    for n in range(4):
        refs[n][at] = slabs_ref[sel[zl * 4 + (x + n) % 4, (zl ^ step) * 4 + x]]


def pack_kernel(ids, hot, sel, x_ref, row_ref, col_ref, *refs):
    r, c = ids[0], ids[1]
    for h in range(2):
        row_ref[h] = x_ref[pl.ds(start(hot[r, h]), B), :].astype(bf16)
        col_ref[h] = x_ref[:, pl.ds(start(hot[c, h]), B)].astype(bf16)
    choose_rows(ids, sel, 0, row_ref, refs)


def pack(ids, hot, sel, value):
    return call(
        pack_kernel,
        (ids, hot, sel),
        (1,),
        [whole((T, T))],
        [whole(s.shape) for s in send_shapes],
        send_shapes,
        (value,),
        moved=5 << 20,
        room=32,
    )


def next_rows(ids, sel, rows, steps):
    count = len(rows)

    def kernel(ids, sel, *refs):
        for m in range(count):
            choose_rows(ids, sel, steps[m], refs[m], refs[count:], m)

    return call(
        kernel,
        (ids, sel),
        (1,),
        [whole(arg.shape) for arg in rows],
        [whole((count, B, T))] * 4,
        [shape((count, B, T))] * 4,
        rows,
        moved=4 << 20,
        room=32,
    )


def choose_cols(ids, sel, here, there):
    def kernel(ids, sel, here_ref, there_ref, out_ref):
        zh, q = ids[1] // 8, ids[1]
        for i in range(8):
            out_ref[2 * i] = here_ref[sel[zh * 8 + i, q]]
            out_ref[2 * i + 1] = there_ref[sel[zh * 8 + i, q ^ 8]]

    return call(
        kernel,
        (ids, sel),
        (1,),
        [whole(here.shape)] * 2,
        whole((16, T, B)),
        shape((16, T, B)),
        (here, there),
        moved=4 << 20,
        room=32,
    )


def over_x(chosen):
    return [chosen[0]] + [permute(chosen[n], x_shift(n)) for n in (1, 2, 3)]


def over_yk(chosen):
    return lax.all_to_all(chosen, ("y", "k"), 0, 0, tiled=True)


def dense_kernel(mirrored):
    def kernel(ids, lists, counts, *refs):
        out_ref, held, total = refs[-3:]
        ham_ref = refs[0]
        r, c = ids[0], ids[1]
        tile = c if mirrored else r
        if mirrored:
            ham_ref = held
            for n in range(4):
                ham_ref[n * 12 : (n + 1) * 12] = refs[n][...]

        def clear(i, carry):
            total[i] = jnp.zeros((B, B), f32)
            return carry

        lax.fori_loop(0, 96, clear, 0)

        def add(slot, carry):
            q = lists[0, tile, slot]
            t = lists[1, tile, slot]
            b = lists[2, tile, slot]
            if mirrored:
                place = q ^ (c // 8 * 8)
                piece = b // 3
                b = ((r + 4 - piece % 4) % 4 * 4 + ((piece // 4) ^ (r // 4))) * 3 + b % 3
            else:
                place = ((q // 4) ^ (r // 4)) * 4 + (r + 4 - q % 4) % 4
            at = t * 16 + place
            total[at] = total[at] + ham_ref[b].astype(f32)
            return carry

        lax.fori_loop(0, counts[tile], add, 0)
        for t in range(6):
            for place in range(16):
                block = total[t * 16 + place].astype(bf16)
                if mirrored:
                    out_ref[place * B : (place + 1) * B, t * B : (t + 1) * B] = block
                else:
                    out_ref[t * B : (t + 1) * B, place * B : (place + 1) * B] = block

    return kernel


def dense(ids, lists, counts, hams, mirrored):
    dims = (2048, T) if mirrored else (T, 2048)
    return call(
        dense_kernel(mirrored),
        (ids, lists, counts),
        (1,),
        [whole(h.shape) for h in hams],
        whole(dims),
        shape(dims),
        hams,
        scratch=[pltpu.VMEM((48, B, B), bf16), pltpu.VMEM((96, B, B), f32)],
        flops=1 << 22,
        moved=5 << 20,
        room=32,
    )


rows = pl.BlockSpec((R, T), lambda i, *_: (i, 0))


def first_products_kernel(second):
    def kernel(ham_t_ref, ham_ref, x_ref, dr_ref, dc_ref, *refs):
        yk_ref = refs[8]
        out_ref, wide = refs[-2:]
        for i in range(16):
            at = i % 2 * 8 + i // 2
            wide[:, at * B : (at + 1) * B] = yk_ref[i]
        near = jnp.concatenate(
            [ref[0] for ref in refs[:4]] + [ref[m] for m in range(2) for ref in refs[4:8]], axis=0
        )
        total = jnp.dot(wide[...], ham_t_ref[...], preferred_element_type=f32) + jnp.dot(
            ham_ref[...], near, preferred_element_type=f32
        )
        total = total + (dr_ref[...] + dc_ref[...] - center) * x_ref[...]
        if second:
            total = total - refs[9][...] * (0.5 / scale)
        out_ref[...] = total

    return kernel


def first_products(ham_t, ham, value, dr, dc, x0, x12, yk, before=None):
    extra = () if before is None else (before,)
    return call(
        first_products_kernel(before is not None),
        (),
        (T // R,),
        [
            whole((2048, T)),
            pl.BlockSpec((R, 1536), lambda i, *_: (i, 0)),
            rows,
            pl.BlockSpec((R, 1), lambda i, *_: (i, 0)),
            whole((1, T)),
        ]
        + [whole(s.shape) for s in x0 + x12]
        + [pl.BlockSpec((16, R, B), lambda i, *_: (0, i, 0))]
        + [rows] * len(extra),
        rows,
        free_shape((T, T), f32),
        (ham_t, ham, value, dr, dc, *x0, *x12, yk, *extra),
        scratch=[pltpu.VMEM((R, 2048), bf16)],
        flops=2 * T * T * 3584,
        moved=20 << 20,
        room=36,
        pinned=True,
    )


def hot_kernel(ids, hot, sel, part_ref, ham_ref, *refs):
    slabs, row_ref, col_ref = refs[:4], refs[4], refs[5]
    r, c = ids[0], ids[1]
    stacked = jnp.concatenate([ref[0] for ref in slabs], axis=0)
    for h in range(2):
        at = pl.ds(start(hot[r, h]), B)
        total = part_ref[at, :] + jnp.dot(ham_ref[at, :], stacked, preferred_element_type=f32)
        row_ref[h] = (total * scale).astype(bf16)
        at = pl.ds(start(hot[c, h]), B)
        some = jnp.concatenate([ref[0, :, at] for ref in slabs], axis=0)
        total = part_ref[:, at] + jnp.dot(ham_ref[...], some, preferred_element_type=f32)
        col_ref[h] = (total * scale).astype(bf16)
    choose_rows(ids, sel, 0, row_ref, refs[6:])


def finish_hot(ids, hot, sel, part, ham, slabs):
    return call(
        hot_kernel,
        (ids, hot, sel),
        (1,),
        [whole((T, T)), pl.BlockSpec((T, 512), lambda i, *_: (0, 3))] + [whole((1, B, T))] * 4,
        [whole(s.shape) for s in send_shapes],
        send_shapes,
        (part, ham, *slabs),
        flops=2 * T * 512 * 512,
        moved=6 << 20,
        room=32,
    )


def finish_kernel(factor):
    def kernel(part_ref, ham_ref, *refs):
        stacked = jnp.concatenate([ref[0] for ref in refs[:4]], axis=0)
        total = part_ref[...] + jnp.dot(ham_ref[...], stacked, preferred_element_type=f32)
        refs[4][...] = total * factor

    return kernel


def finish(part, ham, slabs, factor):
    return call(
        finish_kernel(factor),
        (),
        (T // R,),
        [rows, pl.BlockSpec((R, 512), lambda i, *_: (i, 3))] + [whole((1, B, T))] * 4,
        rows,
        shape((T, T), f32),
        (part, ham, *slabs),
        flops=2 * T * T * 512,
        moved=6 << 20,
        room=32,
    )


def body(start_vector, ham_blocks, diagonal, lists, counts, hot, sel):
    row_index = lax.axis_index("zl") * 4 + lax.axis_index("x")
    col_index = (lax.axis_index("zh") * 4 + lax.axis_index("y")) * 2 + lax.axis_index("k")
    ids = jnp.stack([row_index, col_index]).astype(jnp.int32)
    dr = lax.dynamic_slice_in_dim(diagonal, row_index * T, T).reshape(T, 1)
    dc = lax.dynamic_slice_in_dim(diagonal, col_index * T, T).reshape(1, T)

    piece = lax.dynamic_slice_in_dim(ham_blocks, col_index * 3, 3).transpose(0, 2, 1)
    row, col, *sends = pack(ids, hot, sel, start_vector)
    zh = permute(col, zh_flip)
    piece = permute(after(piece, row), mirror)
    near = over_x(sends)
    pieces = [piece, permute(after(piece, [zh, near[3]]), z_xor(1))]
    pieces += [permute(after(piece, near[n - 1]), z_xor(n)) for n in (2, 3)]
    ham = dense(ids, lists, counts, (ham_blocks,), False)
    quarter, row, col, zh, near = barrier(jnp.concatenate(pieces), row, col, zh, near)
    ham_t = None
    outs = []
    value = start_vector
    for step in range(2):
        first = step == 0
        if not first:
            zh = permute(col, zh_flip)
            near = over_x(sends)
            row, col, zh, near, value = barrier(row, col, zh, near, value)
            outs.append(value)
        z1 = permute(row, z_xor(1))
        z2 = permute(row, z_xor(2))
        yk = over_yk(choose_cols(ids, sel, col, zh))
        hams = over_x([quarter] * 4) if first else []
        far = next_rows(ids, sel, [z1, z2], (1, 2))
        row, far, hams, ham, dr, dc = barrier(row, far, hams, ham, dr, dc)
        z3 = permute(row, z_xor(3))
        x12 = over_x(far)
        if first:
            ham_t = dense(ids, lists, counts, hams, True)
        far = next_rows(ids, sel, [z3], (3,))
        far, x12, ham_t = barrier(far, x12, ham_t)
        x3 = over_x(far)
        before = () if first else (start_vector,)
        part = first_products(ham_t, ham, value, dr, dc, near, x12, yk, *before)
        if first:
            row, col, *sends = finish_hot(ids, hot, sel, part, ham, x3)
            value = finish(part, ham, x3, scale)
        else:
            outs.append(finish(part, ham, x3, 2.0 * scale))
    return tuple(outs)


def solution(mesh):
    fine = Mesh(mesh.devices.reshape(sizes), axes)
    rows, cols = ("zl", "x"), ("zh", "y", "k")
    in_specs = (P(rows, cols), P(rows, None, None), P(), P(), P(), P(), P())
    out_specs = (P(rows, cols), P(rows, cols))
    return jax.shard_map(body, mesh=fine, in_specs=in_specs, out_specs=out_specs, check_vma=False)
```

```python
import jax
import jax.numpy as jnp
from jax import lax
from jax.experimental import pallas as pl
from jax.experimental.pallas import tpu as pltpu
from jax.sharding import Mesh, PartitionSpec as P
import numpy as np

center = 0.25
scale = 1.0 / 2.5
axes = ("zl", "x", "zh", "y", "k")
sizes = (4, 4, 2, 4, 2)
B = 128
T = 768
R = 256
bf16 = jnp.bfloat16
f32 = jnp.float32


def permute(value, target):
    places = list(np.ndindex(*sizes))
    pairs = [
        (int(np.ravel_multi_index(p, sizes)), int(np.ravel_multi_index(target(*p), sizes)))
        for p in places
    ]
    return lax.ppermute(value, axes, pairs)


def z_xor(n):
    return lambda zl, x, zh, y, k: (zl ^ n, x, zh, y, k)


def x_shift(n):
    return lambda zl, x, zh, y, k: (zl, (x + n) % 4, zh, y, k)


def zh_flip(zl, x, zh, y, k):
    return (zl, x, 1 - zh, y, k)


def mirror(zl, x, zh, y, k):
    r, c = zl * 4 + x, zh * 8 + y * 2 + k
    return (c // 4, c % 4, r // 8, (r % 8) // 2, r % 2)


def barrier(*values):
    return lax.optimization_barrier(values)


def after(value, earlier):
    return barrier(value, earlier)[0]


def start(block):
    return pl.multiple_of(block * B, B)


def call(kernel, scalars, grid, in_specs, out_specs, out_shape, args, scratch=(), flops=0, moved=0, room=1, pinned=False):
    return pl.pallas_call(
        kernel,
        grid_spec=pltpu.PrefetchScalarGridSpec(
            num_scalar_prefetch=len(scalars),
            grid=grid,
            in_specs=in_specs,
            out_specs=out_specs,
            scratch_shapes=list(scratch),
        ),
        out_shape=out_shape,
        compiler_params=pltpu.CompilerParams(vmem_limit_bytes=room << 20),
        cost_estimate=pl.CostEstimate(flops=flops, bytes_accessed=moved, transcendentals=0),
    )(*scalars, *(pltpu.with_memory_space_constraint(arg, pltpu.HBM) if pinned else arg for arg in args))


def shape(dims, kind=bf16):
    return pltpu.HBM(dims, kind)


def free_shape(dims, kind=bf16):
    return jax.ShapeDtypeStruct(dims, kind)


def whole(dims):
    return pl.BlockSpec(dims, lambda i, *_: (0,) * len(dims))


send_shapes = [shape((2, B, T)), shape((2, T, B))] + [shape((1, B, T))] * 4


def choose_rows(ids, sel, step, slabs_ref, refs, at=0):
    zl, x = ids[0] // 4, ids[0] % 4
    for n in range(4):
        refs[n][at] = slabs_ref[sel[zl * 4 + (x + n) % 4, (zl ^ step) * 4 + x]]


def pack_kernel(ids, hot, sel, x_ref, row_ref, col_ref, *refs):
    r, c = ids[0], ids[1]
    for h in range(2):
        row_ref[h] = x_ref[pl.ds(start(hot[r, h]), B), :].astype(bf16)
        col_ref[h] = x_ref[:, pl.ds(start(hot[c, h]), B)].astype(bf16)
    choose_rows(ids, sel, 0, row_ref, refs)


def pack(ids, hot, sel, value):
    return call(
        pack_kernel,
        (ids, hot, sel),
        (1,),
        [whole((T, T))],
        [whole(s.shape) for s in send_shapes],
        send_shapes,
        (value,),
        moved=5 << 20,
        room=32,
    )


def next_rows(ids, sel, rows, steps):
    count = len(rows)

    def kernel(ids, sel, *refs):
        for m in range(count):
            choose_rows(ids, sel, steps[m], refs[m], refs[count:], m)

    return call(
        kernel,
        (ids, sel),
        (1,),
        [whole(arg.shape) for arg in rows],
        [whole((count, B, T))] * 4,
        [shape((count, B, T))] * 4,
        rows,
        moved=4 << 20,
        room=32,
    )


def choose_cols(ids, sel, here, there):
    def kernel(ids, sel, here_ref, there_ref, out_ref):
        zh, q = ids[1] // 8, ids[1]
        for i in range(8):
            out_ref[2 * i] = here_ref[sel[zh * 8 + i, q]]
            out_ref[2 * i + 1] = there_ref[sel[zh * 8 + i, q ^ 8]]

    return call(
        kernel,
        (ids, sel),
        (1,),
        [whole(here.shape)] * 2,
        whole((16, T, B)),
        shape((16, T, B)),
        (here, there),
        moved=4 << 20,
        room=32,
    )


def over_x(chosen):
    return [chosen[0]] + [permute(chosen[n], x_shift(n)) for n in (1, 2, 3)]


def over_yk(chosen):
    return lax.all_to_all(chosen, ("y", "k"), 0, 0, tiled=True)


def dense_kernel(mirrored):
    def kernel(ids, lists, counts, *refs):
        out_ref, held, total = refs[-3:]
        ham_ref = refs[0]
        r, c = ids[0], ids[1]
        tile = c if mirrored else r
        if mirrored:
            ham_ref = held
            for n in range(4):
                ham_ref[n * 12 : (n + 1) * 12] = refs[n][...]

        def clear(i, carry):
            total[i] = jnp.zeros((B, B), f32)
            return carry

        lax.fori_loop(0, 96, clear, 0)

        def add(slot, carry):
            q = lists[0, tile, slot]
            t = lists[1, tile, slot]
            b = lists[2, tile, slot]
            if mirrored:
                place = q ^ (c // 8 * 8)
                piece = b // 3
                b = ((r + 4 - piece % 4) % 4 * 4 + ((piece // 4) ^ (r // 4))) * 3 + b % 3
            else:
                place = ((q // 4) ^ (r // 4)) * 4 + (r + 4 - q % 4) % 4
            at = t * 16 + place
            total[at] = total[at] + ham_ref[b].astype(f32)
            return carry

        lax.fori_loop(0, counts[tile], add, 0)
        for t in range(6):
            for place in range(16):
                block = total[t * 16 + place].astype(bf16)
                if mirrored:
                    out_ref[place * B : (place + 1) * B, t * B : (t + 1) * B] = block
                else:
                    out_ref[t * B : (t + 1) * B, place * B : (place + 1) * B] = block

    return kernel


def dense(ids, lists, counts, hams, mirrored):
    dims = (2048, T) if mirrored else (T, 2048)
    return call(
        dense_kernel(mirrored),
        (ids, lists, counts),
        (1,),
        [whole(h.shape) for h in hams],
        whole(dims),
        shape(dims),
        hams,
        scratch=[pltpu.VMEM((48, B, B), bf16), pltpu.VMEM((96, B, B), f32)],
        flops=1 << 22,
        moved=5 << 20,
        room=32,
    )


rows = pl.BlockSpec((R, T), lambda i, *_: (i, 0))


def first_products_kernel(second):
    def kernel(ham_t_ref, ham_ref, x_ref, dr_ref, dc_ref, *refs):
        yk_ref = refs[8]
        out_ref, wide = refs[-2:]
        for i in range(16):
            at = i % 2 * 8 + i // 2
            wide[:, at * B : (at + 1) * B] = yk_ref[i]
        near = jnp.concatenate(
            [ref[0] for ref in refs[:4]] + [ref[m] for m in range(2) for ref in refs[4:8]], axis=0
        )
        total = jnp.dot(wide[...], ham_t_ref[...], preferred_element_type=f32) + jnp.dot(
            ham_ref[...], near, preferred_element_type=f32
        )
        total = total + (dr_ref[...] + dc_ref[...] - center) * x_ref[...]
        if second:
            total = total - refs[9][...] * (0.5 / scale)
        out_ref[...] = total

    return kernel


def first_products(ham_t, ham, value, dr, dc, x0, x12, yk, before=None):
    extra = () if before is None else (before,)
    return call(
        first_products_kernel(before is not None),
        (),
        (T // R,),
        [
            whole((2048, T)),
            pl.BlockSpec((R, 1536), lambda i, *_: (i, 0)),
            rows,
            pl.BlockSpec((R, 1), lambda i, *_: (i, 0)),
            whole((1, T)),
        ]
        + [whole(s.shape) for s in x0 + x12]
        + [pl.BlockSpec((16, R, B), lambda i, *_: (0, i, 0))]
        + [rows] * len(extra),
        rows,
        free_shape((T, T), f32),
        (ham_t, ham, value, dr, dc, *x0, *x12, yk, *extra),
        scratch=[pltpu.VMEM((R, 2048), bf16)],
        flops=2 * T * T * 3584,
        moved=20 << 20,
        room=36,
        pinned=True,
    )


def hot_kernel(ids, hot, sel, part_ref, ham_ref, *refs):
    slabs, row_ref, col_ref = refs[:4], refs[4], refs[5]
    r, c = ids[0], ids[1]
    stacked = jnp.concatenate([ref[0] for ref in slabs], axis=0)
    for h in range(2):
        at = pl.ds(start(hot[r, h]), B)
        total = part_ref[at, :] + jnp.dot(ham_ref[at, :], stacked, preferred_element_type=f32)
        row_ref[h] = (total * scale).astype(bf16)
        at = pl.ds(start(hot[c, h]), B)
        some = jnp.concatenate([ref[0, :, at] for ref in slabs], axis=0)
        total = part_ref[:, at] + jnp.dot(ham_ref[...], some, preferred_element_type=f32)
        col_ref[h] = (total * scale).astype(bf16)
    choose_rows(ids, sel, 0, row_ref, refs[6:])


def finish_hot(ids, hot, sel, part, ham, slabs):
    return call(
        hot_kernel,
        (ids, hot, sel),
        (1,),
        [whole((T, T)), pl.BlockSpec((T, 512), lambda i, *_: (0, 3))] + [whole((1, B, T))] * 4,
        [whole(s.shape) for s in send_shapes],
        send_shapes,
        (part, ham, *slabs),
        flops=2 * T * 512 * 512,
        moved=6 << 20,
        room=32,
    )


def finish_kernel(factor):
    def kernel(part_ref, ham_ref, *refs):
        stacked = jnp.concatenate([ref[0] for ref in refs[:4]], axis=0)
        total = part_ref[...] + jnp.dot(ham_ref[...], stacked, preferred_element_type=f32)
        refs[4][...] = total * factor

    return kernel


def finish(part, ham, slabs, factor):
    return call(
        finish_kernel(factor),
        (),
        (T // R,),
        [rows, pl.BlockSpec((R, 512), lambda i, *_: (i, 3))] + [whole((1, B, T))] * 4,
        rows,
        shape((T, T), f32),
        (part, ham, *slabs),
        flops=2 * T * T * 512,
        moved=6 << 20,
        room=32,
    )


def body(start_vector, ham_blocks, diagonal, lists, counts, hot, sel):
    row_index = lax.axis_index("zl") * 4 + lax.axis_index("x")
    col_index = (lax.axis_index("zh") * 4 + lax.axis_index("y")) * 2 + lax.axis_index("k")
    ids = jnp.stack([row_index, col_index]).astype(jnp.int32)
    dr = lax.dynamic_slice_in_dim(diagonal, row_index * T, T).reshape(T, 1)
    dc = lax.dynamic_slice_in_dim(diagonal, col_index * T, T).reshape(1, T)

    piece = lax.dynamic_slice_in_dim(ham_blocks, col_index * 3, 3).transpose(0, 2, 1)
    piece = permute(piece, mirror)
    row, col, *sends = pack(ids, hot, sel, after(start_vector, piece))
    zh = permute(col, zh_flip)
    near = over_x(sends)
    pieces = [piece, permute(after(piece, [zh, near[3]]), z_xor(1))]
    pieces += [permute(after(piece, near[n - 1]), z_xor(n)) for n in (2, 3)]
    ham = dense(ids, lists, counts, (ham_blocks,), False)
    quarter, row, col, zh, near = barrier(jnp.concatenate(pieces), row, col, zh, near)
    ham_t = None
    outs = []
    value = start_vector
    for step in range(2):
        first = step == 0
        if not first:
            zh = permute(col, zh_flip)
            near = over_x(sends)
            row, col, zh, near, value = barrier(row, col, zh, near, value)
            outs.append(value)
        z1 = permute(row, z_xor(1))
        z2 = permute(row, z_xor(2))
        yk = over_yk(choose_cols(ids, sel, col, zh))
        hams = over_x([quarter] * 4) if first else []
        far = next_rows(ids, sel, [z1, z2], (1, 2))
        row, far, hams, ham, dr, dc = barrier(row, far, hams, ham, dr, dc)
        z3 = permute(row, z_xor(3))
        x12 = over_x(far)
        if first:
            ham_t = dense(ids, lists, counts, hams, True)
        far = next_rows(ids, sel, [z3], (3,))
        far, x12, ham_t = barrier(far, x12, ham_t)
        x3 = over_x(far)
        before = () if first else (start_vector,)
        part = first_products(ham_t, ham, value, dr, dc, near, x12, yk, *before)
        if first:
            row, col, *sends = finish_hot(ids, hot, sel, part, ham, x3)
            value = finish(part, ham, x3, scale)
        else:
            outs.append(finish(part, ham, x3, 2.0 * scale))
    return tuple(outs)


def solution(mesh):
    fine = Mesh(mesh.devices.reshape(sizes), axes)
    rows, cols = ("zl", "x"), ("zh", "y", "k")
    in_specs = (P(rows, cols), P(rows, None, None), P(), P(), P(), P(), P())
    out_specs = (P(rows, cols), P(rows, cols))
    return jax.shard_map(body, mesh=fine, in_specs=in_specs, out_specs=out_specs, check_vma=False)
```
